128 devices in a mesh: row: 8 (over y_hi, x), col: 16 (over y_lo, z, core).
Axes of the slice: x: 4, y: 4 (y_hi: 2, y_lo: 2; y = y_hi * 2 + y_lo), z: 4, core: 2. Of those that a mesh axis runs over, the one named last changes fastest.
Arguments:
- right_side: float32 [16, 512, 512], P('col', 'row'), may hold values from -6 to 6
- affinity_blocks: float32 [16, 16, 8, 128, 128], P('row', 'col'), may hold values from -0.03125 to 0.03125
- block_coords: int32 [16, 16, 8, 2], P('row', 'col'), may hold values from 0 to 3
- block_counts: int32 [16, 16], P('row', 'col'), may hold values from 4 to 8, as said below
Outputs:
- ranking: float32 [16, 512, 512], P('col', 'row')
- residual: float32 [16, 512, 512], P('col', 'row')
The draws below stay inside these ranges and needn't reach their ends.
Inputs may be any that keep to these rules, and one draw needn't show every extreme that they name: `block_counts`: some grid tile holds 8 live blocks in every draw.
All inputs are finite; a program needn't handle non-finite values.
Results may differ from the reference program's by a relative error of at most 0.0003.
Values sent between devices are 32-bit elements; how exact they have to be, the bound alone decides.
No kernel may reach another device: no remote copies, remote signals or barrier semaphores. Data moves between devices by JAX's collectives and lax.ppermute only.
A program may use at most 64 MiB of HBM per device.

```python
import jax
import jax.numpy as jnp
from jax import lax

W = 512
BLK = 128
BT = 4
ITERS = 3
GRID = 16
TILE = 512
NBLK = 8


def draw_block_counts(key, part):
    lowest = (NBLK + 1) // 2
    counts = jax.random.randint(jax.random.fold_in(key, 11), (GRID * GRID,), lowest, NBLK + 1)
    chosen = jax.random.randint(jax.random.fold_in(key, 12), (), 0, GRID * GRID)
    counts = jnp.where(jnp.arange(GRID * GRID) == chosen, NBLK, counts)
    return counts.reshape(GRID, GRID).astype(jnp.int32)


def touch_ends(array, key, smallest, top_value):
    dims = array.shape
    spot = [jax.random.randint(jax.random.fold_in(key, axis), (), 0, dims[axis]) for axis in range(len(dims))]
    array = array.at[tuple(spot)].set(smallest)
    longest = dims.index(max(dims))
    spot[longest] = (spot[longest] + 1) % dims[longest]
    return array.at[tuple(spot)].set(top_value)


def block_levels(rng, extent, split, low, high):
    level, own = 1.0, jax.random.fold_in(rng, 6)
    for dim, parts in split:
        draws = jnp.exp(jax.random.uniform(jax.random.fold_in(own, dim), (parts,), jnp.float32, low / len(split), high / len(split)))
        level = level * jnp.repeat(draws, extent[dim] // parts).reshape([-1 if axis == dim else 1 for axis in range(len(extent))])
    return level


def scatter_about(key, extent, width, reach, split=(), kind=jnp.bfloat16):
    level = block_levels(key, extent, split, -0.22, 0.18) if split else 1.0
    values = jax.random.normal(key, extent, jnp.float32) * width * level
    return jnp.minimum(jnp.maximum(values, -reach), reach).astype(kind)


def setup_inputs(seed: int = 0) -> dict:
    key_of = jax.random.split(jax.random.key(seed), 5)
    return {
        "right_side": scatter_about(key_of[0], (GRID, TILE, W), 1.0, 6.0, ((0, 16), (1, 8)), jnp.float32),
        "affinity_blocks": scatter_about(key_of[1], (GRID, GRID, NBLK, BLK, BLK), (8 * GRID * NBLK * BLK // BT) ** -0.5, 0.03125, ((0, 8), (1, 16)), jnp.float32),
        "block_coords": touch_ends(jax.random.randint(key_of[2], (GRID, GRID, NBLK, 2), 0, BT), jax.random.fold_in(key_of[2], 1), 0, BT - 1).astype(jnp.int32),
        "block_counts": draw_block_counts(jax.random.fold_in(key_of[4], 71), 0),
    }


diffusion = 0.8


def live_blocks(blocks, count):
    live = (jnp.arange(blocks.shape[0], dtype=jnp.int32) < count.astype(jnp.int32)).astype(blocks.dtype)
    return blocks * live[:, None, None]


def tile_products(masked, rows, cols, column_field, row_field):
    position = jnp.arange(column_field.shape[0], dtype=jnp.int32)
    picked = jnp.take(column_field, cols.astype(jnp.int32), axis=0)
    product = jnp.einsum('kab,kbw->kaw', masked, picked, precision=lax.Precision.HIGHEST)
    row_onehot = (rows.astype(jnp.int32)[None, :] == position[:, None]).astype(masked.dtype)
    forward = jnp.einsum('tk,kaw->taw', row_onehot, product, precision=lax.Precision.HIGHEST)
    chosen = jnp.take(row_field, rows.astype(jnp.int32), axis=0)
    mirrored = jnp.einsum('kab,kaw->kbw', masked, chosen, precision=lax.Precision.HIGHEST)
    col_onehot = (cols.astype(jnp.int32)[None, :] == position[:, None]).astype(masked.dtype)
    backward = jnp.einsum('tk,kbw->tbw', col_onehot, mirrored, precision=lax.Precision.HIGHEST)
    return forward, backward


def operate(field, affinity_blocks, block_coords, block_counts):
    grid_count = field.shape[0]
    blocked = field.reshape(grid_count, BT, BLK, W)

    def visit(index, total):
        index = jnp.asarray(index).astype(jnp.int32)
        row_tile = index // grid_count
        col_tile = index % grid_count
        masked = live_blocks(affinity_blocks[row_tile, col_tile], block_counts[row_tile, col_tile])
        coords = block_coords[row_tile, col_tile]
        forward, backward = tile_products(masked, coords[:, 0], coords[:, 1], blocked[col_tile], blocked[row_tile])
        total = total.at[row_tile].add(forward)
        total = total.at[col_tile].add(backward)
        return total

    total = lax.fori_loop(0, grid_count * grid_count, visit, jnp.zeros_like(blocked))
    return field - diffusion * total.reshape(field.shape)


def reference(right_side, affinity_blocks, block_coords, block_counts):
    ranking = jnp.zeros_like(right_side)
    residual = right_side
    direction = right_side
    norm_now = jnp.sum(residual * residual, axis=(0, 1))
    for step in range(ITERS):
        image = operate(direction, affinity_blocks, block_coords, block_counts)
        alpha = norm_now / jnp.sum(direction * image, axis=(0, 1))
        ranking = ranking + alpha * direction
        residual = residual - alpha * image
        norm_next = jnp.sum(residual * residual, axis=(0, 1))
        direction = residual + (norm_next / norm_now) * direction
        norm_now = norm_next
    return ranking, residual
```

```python
import functools

import jax
import jax.numpy as jnp
from jax import lax
from jax.experimental import pallas as pl
from jax.experimental.pallas import tpu as pltpu
from jax.sharding import PartitionSpec as P

ITERS = 3
DIFFUSION = 0.8
RC = ("row", "col")


def split_id(device):
    r, c = divmod(device, 16)
    yh, x = divmod(r, 4)
    yl, q = divmod(c, 8)
    return yh * 2 + yl, x, q // 2, q % 2


def device_id(y, x, z, k):
    return ((y // 2) * 4 + x) * 16 + (y % 2) * 8 + z * 2 + k


def groups_by(key):
    groups = {}
    for device in range(128):
        groups.setdefault(key(*split_id(device)), []).append(device)
    return list(groups.values())


PLANES = groups_by(lambda y, x, z, k: (y, k))
SHEETS = groups_by(lambda y, x, z, k: (x, k))


def shift_y(d):
    pairs = []
    for device in range(128):
        y, x, z, k = split_id(device)
        pairs.append((device, device_id((y + d) % 4, x, z, k)))
    return pairs


SWAP = [(device, device ^ 1) for device in range(128)]


def exchange(send, groups):
    return lax.all_to_all(send, RC, 0, 0, axis_index_groups=groups, tiled=True)


def call(body, limit=16, **kw):
    return pl.pallas_call(
        body, compiler_params=pltpu.CompilerParams(vmem_limit_bytes=limit * 2**20), **kw
    )


def assemble_body(codes, own, left, right, far0, far1, hi, lo, dense):
    step = pl.program_id(0)

    @pl.when(step == 0)
    def _():
        dense[...] = jnp.zeros_like(dense)
        y = codes[64]
        pieces = ((own, 0, 0, 16), (left, 1, 0, 16), (right, 3, 0, 16), (far0, 2, 0, 8), (far1, 2, 8, 8))
        for ref, shift, first, count in pieces:
            base = ((y - shift) & 3) * 16 + first

            def put(b, carry, ref=ref, base=base):
                code = codes[base + b]

                @pl.when(code >= 0)
                def _():
                    ro = pl.multiple_of((code >> 3) * 128, 128)
                    co = pl.multiple_of((code & 7) * 128, 128)
                    dense[pl.ds(ro, 128), pl.ds(co, 128)] += ref[b]

                return carry

            lax.fori_loop(0, count, put, 0)

    def narrow(i, carry):
        rows = pl.ds(pl.multiple_of(i * 32, 32), 32)
        value = dense[pl.ds(pl.multiple_of(step * 256 + i * 32, 32), 32), :]
        top = value.astype(jnp.bfloat16)
        hi[rows, :] = top
        lo[rows, :] = (value - top.astype(jnp.float32)).astype(jnp.bfloat16)
        return carry

    lax.fori_loop(0, 8, narrow, 0)


def whole(*shape):
    return pl.BlockSpec(shape, lambda i: (0,) * len(shape))


def assemble(codes, own, left, right, far0, far1):
    half = jax.ShapeDtypeStruct((2048, 1024), jnp.bfloat16)
    return call(
        assemble_body,
        limit=26,
        grid=(8,),
        out_shape=(half, half),
        in_specs=[pl.BlockSpec(memory_space=pltpu.SMEM)]
        + [whole(16, 128, 128)] * 3
        + [whole(8, 128, 128)] * 2,
        out_specs=(pl.BlockSpec((256, 1024), lambda i: (i, 0)),) * 2,
        scratch_shapes=[pltpu.VMEM((2048, 1024), jnp.float32)],
        name="assemble",
    )(codes, own, left, right, far0, far1)


def parted(value):
    top = value.astype(jnp.bfloat16)
    return top, (value - top.astype(jnp.float32)).astype(jnp.bfloat16)


def dot(a, b):
    return jnp.dot(a, b, preferred_element_type=jnp.float32)


def chunk(ref, j):
    return ref[:, pl.ds(j * 16, 16), :].reshape(256, 128)


def part_right(recv, right):
    for s in range(4):
        top, rest = parted(chunk(recv, 4 + s))
        right[pl.ds(s * 256, 256), :128] = top
        right[pl.ds(s * 256, 256), 128:] = rest


def forward(hi, lo, right):
    wide = dot(hi[...], right[...])
    return wide[:, :128] + wide[:, 128:] + dot(lo[...], right[:, :128])


def mate_body(recv, hi, lo, out, right):
    @pl.when(pl.program_id(0) == 0)
    def _():
        part_right(recv, right)

    out[...] = forward(hi, lo, right)


def rows_at(first):
    return pl.BlockSpec((512, 1024), lambda i: (first + i, 0))


def mate(recv, hi, lo):
    return call(
        mate_body,
        grid=(2,),
        out_shape=jax.ShapeDtypeStruct((1024, 128), jnp.float32),
        in_specs=[whole(16, 128, 128), rows_at(2), rows_at(2)],
        out_specs=pl.BlockSpec((512, 128), lambda i: (i, 0)),
        scratch_shapes=[pltpu.VMEM((1024, 256), jnp.bfloat16)],
        name="mate",
    )(recv, hi, lo)


def mirror_body(recv, other, hi0, lo0, hi1, lo1, sums, out, scalars, back):
    step = pl.program_id(0)

    @pl.when(step == 0)
    def _():
        back[...] = jnp.zeros_like(back)

    for ref, hi, lo in ((recv, hi0, lo0), (other, hi1, lo1)):
        pairs = [parted(chunk(ref, step * 2 + c).T) for c in range(2)]
        top = jnp.concatenate([pair[0] for pair in pairs], axis=1)
        rest = jnp.concatenate([pair[1] for pair in pairs], axis=1)
        wide = dot(jnp.concatenate([top, rest], axis=0), hi[...])
        back[...] += wide[:128] + wide[128:] + dot(top, lo[...])

    @pl.when(step == 1)
    def _():
        out[...] = back[...].T
        curve = jnp.zeros((8, 128), jnp.float32)
        for s in range(4):
            piece = chunk(recv, 4 + s) * out[s * 256 : (s + 1) * 256]
            curve = curve + jnp.sum(piece.reshape(32, 8, 128), axis=0)
        place = lax.broadcasted_iota(jnp.int32, (8, 128), 0)
        scalars[...] = jnp.where(place == 2, row_sum(curve) * (2 * DIFFUSION), sums[...])


def mirror(recv, other, hi, lo, sums):
    return call(
        mirror_body,
        grid=(2,),
        limit=20,
        out_shape=(
            jax.ShapeDtypeStruct((1024, 128), jnp.float32),
            jax.ShapeDtypeStruct((8, 128), jnp.float32),
        ),
        in_specs=[whole(16, 128, 128)] * 2
        + [rows_at(0), rows_at(0), rows_at(2), rows_at(2), whole(8, 128)],
        out_specs=(whole(1024, 128), whole(8, 128)),
        scratch_shapes=[pltpu.VMEM((128, 1024), jnp.float32)],
        name="mirror",
    )(recv, other, hi, lo, hi, lo, sums)


def gathered_body(recv, hi, lo, theirs, mirrored, mine, mates, out, right):
    step = pl.program_id(0)

    @pl.when(step == 0)
    def _():
        part_right(recv, right)
        for s in range(4):
            out[:, 64 + s * 16 : 80 + s * 16, :] = mirrored[s * 256 : (s + 1) * 256].reshape(16, 16, 128)

    part = forward(hi, lo, right) + theirs[...]
    for c in range(2):
        j = step * 2 + c
        piece = part[c * 256 : (c + 1) * 256]
        out[:, pl.ds(j * 16, 16), :] = piece.reshape(16, 16, 128)

    @pl.when(step == 1)
    def _():
        row = mine[...] + mates[...]
        out[:, 128:136, :] = jnp.broadcast_to(row[None], (16, 8, 128))


def gathered(recv, hi, lo, theirs, mirrored, mine, mates):
    return call(
        gathered_body,
        grid=(2,),
        out_shape=jax.ShapeDtypeStruct((16, 136, 128), jnp.float32),
        in_specs=[
            whole(16, 128, 128),
            rows_at(0),
            rows_at(0),
            pl.BlockSpec((512, 128), lambda i: (i, 0)),
            whole(1024, 128),
            whole(8, 128),
            whole(8, 128),
        ],
        out_specs=whole(16, 136, 128),
        scratch_shapes=[
            pltpu.VMEM((1024, 256), jnp.bfloat16),
        ],
        name="gathered",
    )(recv, hi, lo, theirs, mirrored, mine, mates)


def multiply(recv, sums, hi, lo):
    other = lax.ppermute(recv, RC, SWAP)
    theirs = lax.ppermute(mate(recv, hi, lo), RC, SWAP)
    mirrored, mine = mirror(recv, other, hi, lo, sums)
    mates = lax.ppermute(mine, RC, SWAP)
    return gathered(recv, hi, lo, theirs, mirrored, mine, mates)


def spread(field, send):
    for s in range(4):
        for g in range(4):
            piece = field(s, g)
            for other in range(4):
                send[g * 4 + other, s * 16 : s * 16 + 16, :] = piece
                send[other * 4 + g, 64 + s * 16 : 80 + s * 16, :] = piece


def row_sum(value):
    return jnp.sum(value, axis=0, keepdims=True)


def rows_of(*rows):
    place = lax.broadcasted_iota(jnp.int32, (8, 128), 0)
    out = jnp.zeros((8, 128), jnp.float32)
    for i, row in enumerate(rows):
        out = jnp.where(place == i, row, out)
    return out


def start_body(recv, send, sums):
    square = jnp.zeros((16, 128), jnp.float32)
    for i in range(16):
        piece = recv[i, :16]
        square = square + piece * piece
    spread(lambda s, g: recv[s * 4 + g, :16], send)
    sums[...] = rows_of(row_sum(square))


def start(recv):
    return call(
        start_body,
        out_shape=(
            jax.ShapeDtypeStruct((16, 128, 128), jnp.float32),
            jax.ShapeDtypeStruct((8, 128), jnp.float32),
        ),
        name="start",
    )(recv)


def update_body(step, *refs):
    if step == 0:
        recv, residual = refs[:2]
        outs = refs[2:]
    else:
        recv, residual, direction, image, ranking, last = refs[:6]
        outs = refs[6:]
    total = jnp.zeros((8, 128), jnp.float32)
    for i in range(16):
        total = total + recv[i, 128:136]
    now = total[0:1]
    curve = now - total[2:3]
    if step > 0:
        beta = now / last[0:1]
        curve = curve + 2.0 * beta * total[1:2] + beta * beta * last[1:2]
    alpha = now / curve
    final = step + 1 == ITERS
    square = jnp.zeros((16, 128), jnp.float32)
    cross = jnp.zeros((16, 128), jnp.float32)
    for s in range(4):
        for g in range(4):
            acc = jnp.zeros((16, 128), jnp.float32)
            for other in range(4):
                acc = acc + recv[g * 4 + other, s * 16 : s * 16 + 16]
                acc = acc + recv[other * 4 + g, 64 + s * 16 : 80 + s * 16]
            i = s * 4 + g
            rest = residual[i, :16]
            aim = rest
            made = rest - DIFFUSION * acc
            if step > 0:
                aim = aim + beta * direction[i]
                made = made + beta * image[i]
            ranked = alpha * aim
            if step > 0:
                ranked = ranked + ranking[i]
            rest = rest - alpha * made
            if final:
                outs[0][i, 0] = ranked
                outs[0][i, 1] = rest
            else:
                send, new_residual, new_direction, new_image, new_ranking = outs[:5]
                new_residual[i] = rest
                new_direction[i] = aim
                new_image[i] = made
                new_ranking[i] = ranked
                square = square + rest * rest
                cross = cross + rest * made
    if not final:
        spread(lambda s, g: new_residual[s * 4 + g], send)
        outs[5][...] = rows_of(now, curve)
        outs[6][...] = rows_of(row_sum(square), row_sum(cross))


def update(step, *operands):
    field = jax.ShapeDtypeStruct((16, 16, 128), jnp.float32)
    small = jax.ShapeDtypeStruct((8, 128), jnp.float32)
    if step + 1 == ITERS:
        shapes = [jax.ShapeDtypeStruct((16, 2, 16, 128), jnp.float32)]
    else:
        send = jax.ShapeDtypeStruct((16, 128, 128), jnp.float32)
        shapes = [send, field, field, field, field, small, small]
    return call(
        functools.partial(update_body, step), out_shape=shapes, name="update"
    )(*operands)


def shards(right_side, affinity_blocks, block_coords, block_counts):
    r = lax.axis_index("row")
    c = lax.axis_index("col")
    yh, yl, z, k = r // 4, c // 8, (c // 2) % 4, c % 2
    own = affinity_blocks.reshape(16, 128, 128)
    left = lax.ppermute(own, RC, shift_y(1))
    right = lax.ppermute(own, RC, shift_y(3))

    br = block_coords[:, 0, :, 0]
    bc = block_coords[:, 0, :, 1]
    par = jnp.arange(2, dtype=jnp.int32)[:, None] ^ k
    row128 = par * 8 + ((br // 2) * 2 + yh) * 2 + br % 2
    col128 = ((bc // 2) * 2 + yl) * 2 + bc % 2
    live = jnp.arange(8, dtype=jnp.int32)[None, :] < block_counts
    code = jnp.where(live, row128 * 8 + col128, -1).astype(jnp.float32)
    meta = jnp.pad(code.reshape(1, 16), ((0, 7), (0, 112)))

    send = right_side.reshape(4, 16, 4, 128).transpose(2, 0, 1, 3).reshape(16, 16, 128)
    send = jnp.concatenate([send, jnp.broadcast_to(meta[None], (16, 8, 128))], axis=1)
    recv = exchange(send, SHEETS)
    codes = lax.dynamic_slice(recv.reshape(4, 4, 24, 128), (0, z, 16, 0), (4, 1, 1, 16))
    codes = jnp.concatenate(
        [codes.reshape(64).astype(jnp.int32), (yh * 2 + yl)[None].astype(jnp.int32)]
    )

    send, sums = start(recv)
    state = (recv,)
    send, left, right = lax.optimization_barrier((send, left, right))
    far0 = lax.ppermute(left[:8], RC, shift_y(1))
    far1 = lax.ppermute(right[8:], RC, shift_y(3))
    got = exchange(send, PLANES)
    hi, lo = assemble(codes, own, left, right, far0, far1)
    for step in range(ITERS):
        if step:
            got = exchange(send, PLANES)
        products = exchange(multiply(got, sums, hi, lo), PLANES)
        made = update(step, products, *state)
        if step + 1 < ITERS:
            send, sums = made[0], made[6]
            state = made[1:6]
    done = exchange(made[0], SHEETS)
    done = done.reshape(4, 4, 2, 16, 128).transpose(2, 1, 3, 0, 4).reshape(2, 1, 64, 512)
    return done[0], done[1]


def solution(mesh):
    in_specs = (
        P("col", "row", None),
        P("row", "col", None, None, None),
        P("row", "col", None, None),
        P("row", "col"),
    )
    out_specs = (P("col", "row", None), P("col", "row", None))
    return jax.shard_map(
        shards, mesh=mesh, in_specs=in_specs, out_specs=out_specs, check_vma=False
    )
```

```python
import functools

import jax
import jax.numpy as jnp
from jax import lax
from jax.experimental import pallas as pl
from jax.experimental.pallas import tpu as pltpu
from jax.sharding import PartitionSpec as P

ITERS = 3
DIFFUSION = 0.8
RC = ("row", "col")


def split_id(device):
    r, c = divmod(device, 16)
    yh, x = divmod(r, 4)
    yl, q = divmod(c, 8)
    return yh * 2 + yl, x, q // 2, q % 2


def device_id(y, x, z, k):
    return ((y // 2) * 4 + x) * 16 + (y % 2) * 8 + z * 2 + k


def groups_by(key):
    groups = {}
    for device in range(128):
        groups.setdefault(key(*split_id(device)), []).append(device)
    return list(groups.values())


PLANES = groups_by(lambda y, x, z, k: (y, k))
SHEETS = groups_by(lambda y, x, z, k: (x, k))


def shift_y(d):
    pairs = []
    for device in range(128):
        y, x, z, k = split_id(device)
        pairs.append((device, device_id((y + d) % 4, x, z, k)))
    return pairs


SWAP = [(device, device ^ 1) for device in range(128)]


def exchange(send, groups):
    return lax.all_to_all(send, RC, 0, 0, axis_index_groups=groups, tiled=True)


def call(body, limit=16, **kw):
    return pl.pallas_call(
        body, compiler_params=pltpu.CompilerParams(vmem_limit_bytes=limit * 2**20), **kw
    )


def assemble_body(codes, *refs):
    pieces, recv, (hi, lo, share, dense) = refs[:8], refs[8], refs[9:]
    step = pl.program_id(0)

    @pl.when(step == 0)
    def _():
        share[...] = recv[:, :64, :]
        dense[...] = jnp.zeros_like(dense)
        y = codes[64]
        for i, ref in enumerate(pieces):
            base = ((y - i // 2) & 3) * 16 + (i % 2) * 8

            def put(b, carry, ref=ref, base=base):
                code = codes[base + b]

                @pl.when(code >= 0)
                def _():
                    ro = pl.multiple_of((code >> 3) * 128, 128)
                    co = pl.multiple_of((code & 7) * 128, 128)
                    dense[pl.ds(ro, 128), pl.ds(co, 128)] += ref[b]

                return carry

            lax.fori_loop(0, 8, put, 0)

    def narrow(i, carry):
        rows = pl.ds(pl.multiple_of(i * 32, 32), 32)
        value = dense[pl.ds(pl.multiple_of(step * 256 + i * 32, 32), 32), :]
        top = value.astype(jnp.bfloat16)
        hi[rows, :] = top
        lo[rows, :] = (value - top.astype(jnp.float32)).astype(jnp.bfloat16)
        return carry

    lax.fori_loop(0, 8, narrow, 0)


def whole(*shape):
    return pl.BlockSpec(shape, lambda i: (0,) * len(shape))


def assemble(codes, pieces, recv):
    half = jax.ShapeDtypeStruct((2048, 1024), jnp.bfloat16)
    return call(
        assemble_body,
        limit=26,
        grid=(8,),
        out_shape=(half, half, jax.ShapeDtypeStruct((16, 64, 128), jnp.float32)),
        in_specs=[pl.BlockSpec(memory_space=pltpu.SMEM)]
        + [whole(8, 128, 128)] * 8
        + [whole(16, 128, 128)],
        out_specs=(pl.BlockSpec((256, 1024), lambda i: (i, 0)),) * 2
        + (whole(16, 64, 128),),
        scratch_shapes=[pltpu.VMEM((2048, 1024), jnp.float32)],
        name="assemble",
    )(codes, *pieces, recv)


def parted(value):
    top = value.astype(jnp.bfloat16)
    return top, (value - top.astype(jnp.float32)).astype(jnp.bfloat16)


def dot(a, b):
    return jnp.dot(a, b, preferred_element_type=jnp.float32)


def chunk(ref, j):
    return ref[:, pl.ds(j * 16, 16), :].reshape(256, 128)


def part_right(recv, right):
    for s in range(4):
        top, rest = parted(chunk(recv, 4 + s))
        right[pl.ds(s * 256, 256), :128] = top
        right[pl.ds(s * 256, 256), 128:] = rest


def forward(hi, lo, right):
    wide = dot(hi[...], right[...])
    return wide[:, :128] + wide[:, 128:] + dot(lo[...], right[:, :128])


def mate_body(recv, hi, lo, out, right):
    @pl.when(pl.program_id(0) == 0)
    def _():
        part_right(recv, right)

    out[...] = forward(hi, lo, right)


def rows_at(first):
    return pl.BlockSpec((512, 1024), lambda i: (first + i, 0))


def mate(recv, hi, lo):
    return call(
        mate_body,
        grid=(2,),
        out_shape=jax.ShapeDtypeStruct((1024, 128), jnp.float32),
        in_specs=[whole(16, 128, 128), rows_at(2), rows_at(2)],
        out_specs=pl.BlockSpec((512, 128), lambda i: (i, 0)),
        scratch_shapes=[pltpu.VMEM((1024, 256), jnp.bfloat16)],
        name="mate",
    )(recv, hi, lo)


def mirror_body(recv, other, hi0, lo0, hi1, lo1, sums, out, scalars, back):
    step = pl.program_id(0)

    @pl.when(step == 0)
    def _():
        back[...] = jnp.zeros_like(back)

    for ref, hi, lo in ((recv, hi0, lo0), (other, hi1, lo1)):
        pairs = [parted(chunk(ref, step * 2 + c).T) for c in range(2)]
        top = jnp.concatenate([pair[0] for pair in pairs], axis=1)
        rest = jnp.concatenate([pair[1] for pair in pairs], axis=1)
        wide = dot(jnp.concatenate([top, rest], axis=0), hi[...])
        back[...] += wide[:128] + wide[128:] + dot(top, lo[...])

    @pl.when(step == 1)
    def _():
        out[...] = back[...].T
        curve = jnp.zeros((8, 128), jnp.float32)
        for s in range(4):
            piece = chunk(recv, 4 + s) * out[s * 256 : (s + 1) * 256]
            curve = curve + jnp.sum(piece.reshape(32, 8, 128), axis=0)
        place = lax.broadcasted_iota(jnp.int32, (8, 128), 0)
        scalars[...] = jnp.where(place == 2, row_sum(curve) * (2 * DIFFUSION), sums[...])


def mirror(recv, other, hi, lo, sums):
    return call(
        mirror_body,
        grid=(2,),
        limit=20,
        out_shape=(
            jax.ShapeDtypeStruct((1024, 128), jnp.float32),
            jax.ShapeDtypeStruct((8, 128), jnp.float32),
        ),
        in_specs=[whole(16, 128, 128), whole(*other.shape)]
        + [rows_at(0), rows_at(0), rows_at(2), rows_at(2), whole(8, 128)],
        out_specs=(whole(1024, 128), whole(8, 128)),
        scratch_shapes=[pltpu.VMEM((128, 1024), jnp.float32)],
        name="mirror",
    )(recv, other, hi, lo, hi, lo, sums)


def gathered_body(recv, hi, lo, theirs, mirrored, mine, mates, out, right):
    step = pl.program_id(0)

    @pl.when(step == 0)
    def _():
        part_right(recv, right)
        for s in range(4):
            out[:, 64 + s * 16 : 80 + s * 16, :] = mirrored[s * 256 : (s + 1) * 256].reshape(16, 16, 128)

    part = forward(hi, lo, right) + theirs[...]
    for c in range(2):
        j = step * 2 + c
        piece = part[c * 256 : (c + 1) * 256]
        out[:, pl.ds(j * 16, 16), :] = piece.reshape(16, 16, 128)

    @pl.when(step == 1)
    def _():
        row = mine[...] + mates[...]
        out[:, 128:136, :] = jnp.broadcast_to(row[None], (16, 8, 128))


def gathered(recv, hi, lo, theirs, mirrored, mine, mates):
    return call(
        gathered_body,
        grid=(2,),
        out_shape=jax.ShapeDtypeStruct((16, 136, 128), jnp.float32),
        in_specs=[
            whole(16, 128, 128),
            rows_at(0),
            rows_at(0),
            pl.BlockSpec((512, 128), lambda i: (i, 0)),
            whole(1024, 128),
            whole(8, 128),
            whole(8, 128),
        ],
        out_specs=whole(16, 136, 128),
        scratch_shapes=[
            pltpu.VMEM((1024, 256), jnp.bfloat16),
        ],
        name="gathered",
    )(recv, hi, lo, theirs, mirrored, mine, mates)


def multiply(recv, share, sums, hi, lo):
    other = lax.ppermute(share, RC, SWAP)
    theirs = lax.ppermute(mate(recv, hi, lo), RC, SWAP)
    mirrored, mine = mirror(recv, other, hi, lo, sums)
    mates = lax.ppermute(mine, RC, SWAP)
    return gathered(recv, hi, lo, theirs, mirrored, mine, mates)


def spread(field, send):
    for s in range(4):
        for g in range(4):
            piece = field(s, g)
            for other in range(4):
                send[g * 4 + other, s * 16 : s * 16 + 16, :] = piece
                send[other * 4 + g, 64 + s * 16 : 80 + s * 16, :] = piece


def row_sum(value):
    return jnp.sum(value, axis=0, keepdims=True)


def rows_of(*rows):
    place = lax.broadcasted_iota(jnp.int32, (8, 128), 0)
    out = jnp.zeros((8, 128), jnp.float32)
    for i, row in enumerate(rows):
        out = jnp.where(place == i, row, out)
    return out


def start_body(recv, send, sums):
    square = jnp.zeros((16, 128), jnp.float32)
    for i in range(16):
        piece = recv[i, :16]
        square = square + piece * piece
    spread(lambda s, g: recv[s * 4 + g, :16], send)
    sums[...] = rows_of(row_sum(square))


def start(recv):
    return call(
        start_body,
        out_shape=(
            jax.ShapeDtypeStruct((16, 128, 128), jnp.float32),
            jax.ShapeDtypeStruct((8, 128), jnp.float32),
        ),
        name="start",
    )(recv)


def update_body(step, *refs):
    if step == 0:
        recv, residual = refs[:2]
        outs = refs[2:]
    else:
        recv, residual, direction, image, ranking, last = refs[:6]
        outs = refs[6:]
    total = jnp.zeros((8, 128), jnp.float32)
    for i in range(16):
        total = total + recv[i, 128:136]
    now = total[0:1]
    curve = now - total[2:3]
    if step > 0:
        beta = now / last[0:1]
        curve = curve + 2.0 * beta * total[1:2] + beta * beta * last[1:2]
    alpha = now / curve
    final = step + 1 == ITERS
    square = jnp.zeros((16, 128), jnp.float32)
    cross = jnp.zeros((16, 128), jnp.float32)
    for s in range(4):
        for g in range(4):
            acc = jnp.zeros((16, 128), jnp.float32)
            for other in range(4):
                acc = acc + recv[g * 4 + other, s * 16 : s * 16 + 16]
                acc = acc + recv[other * 4 + g, 64 + s * 16 : 80 + s * 16]
            i = s * 4 + g
            rest = residual[i, :16]
            aim = rest
            made = rest - DIFFUSION * acc
            if step > 0:
                aim = aim + beta * direction[i]
                made = made + beta * image[i]
            ranked = alpha * aim
            if step > 0:
                ranked = ranked + ranking[i]
            rest = rest - alpha * made
            if final:
                outs[0][i, 0] = ranked
                outs[0][i, 1] = rest
            else:
                send, new_residual, new_direction, new_image, new_ranking = outs[:5]
                new_residual[i] = rest
                new_direction[i] = aim
                new_image[i] = made
                new_ranking[i] = ranked
                square = square + rest * rest
                cross = cross + rest * made
    if not final:
        spread(lambda s, g: new_residual[s * 4 + g], send)
        outs[5][...] = rows_of(now, curve)
        outs[6][...] = rows_of(row_sum(square), row_sum(cross))


def update(step, *operands):
    field = jax.ShapeDtypeStruct((16, 16, 128), jnp.float32)
    small = jax.ShapeDtypeStruct((8, 128), jnp.float32)
    if step + 1 == ITERS:
        shapes = [jax.ShapeDtypeStruct((16, 2, 16, 128), jnp.float32)]
    else:
        send = jax.ShapeDtypeStruct((16, 128, 128), jnp.float32)
        shapes = [send, field, field, field, field, small, small]
    return call(
        functools.partial(update_body, step), out_shape=shapes, name="update"
    )(*operands)


def shards(right_side, affinity_blocks, block_coords, block_counts):
    r = lax.axis_index("row")
    c = lax.axis_index("col")
    yh, yl, z, k = r // 4, c // 8, (c // 2) % 4, c % 2
    own0 = affinity_blocks[0, 0]
    own1 = affinity_blocks[1, 0]
    left0 = lax.ppermute(own0, RC, shift_y(1))
    right1 = lax.ppermute(own1, RC, shift_y(3))

    br = block_coords[:, 0, :, 0]
    bc = block_coords[:, 0, :, 1]
    par = jnp.arange(2, dtype=jnp.int32)[:, None] ^ k
    row128 = par * 8 + ((br // 2) * 2 + yh) * 2 + br % 2
    col128 = ((bc // 2) * 2 + yl) * 2 + bc % 2
    live = jnp.arange(8, dtype=jnp.int32)[None, :] < block_counts
    code = jnp.where(live, row128 * 8 + col128, -1).astype(jnp.float32)
    meta = jnp.pad(code.reshape(1, 16), ((0, 7), (0, 112)))

    send = right_side.reshape(4, 16, 4, 128).transpose(2, 0, 1, 3).reshape(16, 16, 128)
    send = jnp.concatenate([send, jnp.broadcast_to(meta[None], (16, 8, 128))], axis=1)
    recv = exchange(send, SHEETS)
    codes = lax.dynamic_slice(recv.reshape(4, 4, 24, 128), (0, z, 16, 0), (4, 1, 1, 16))
    codes = jnp.concatenate(
        [codes.reshape(64).astype(jnp.int32), (yh * 2 + yl)[None].astype(jnp.int32)]
    )

    send, sums = start(recv)
    state = (recv,)
    send, left0, right1 = lax.optimization_barrier((send, left0, right1))
    later0, later1, recv = lax.optimization_barrier((own0, own1, recv))
    far0 = lax.ppermute(left0, RC, shift_y(1))
    far1 = lax.ppermute(right1, RC, shift_y(3))
    left1 = lax.ppermute(later1, RC, shift_y(1))
    right0 = lax.ppermute(later0, RC, shift_y(3))
    got = exchange(send, PLANES)
    pieces = (own0, own1, left0, left1, far0, far1, right0, right1)
    hi, lo, share = assemble(codes, pieces, got)
    for step in range(ITERS):
        if step:
            got = share = exchange(send, PLANES)
        products = exchange(multiply(got, share, sums, hi, lo), PLANES)
        made = update(step, products, *state)
        if step + 1 < ITERS:
            send, sums = made[0], made[6]
            state = made[1:6]
    done = exchange(made[0], SHEETS)
    done = done.reshape(4, 4, 2, 16, 128).transpose(2, 1, 3, 0, 4).reshape(2, 1, 64, 512)
    return done[0], done[1]


def solution(mesh):
    in_specs = (
        P("col", "row", None),
        P("row", "col", None, None, None),
        P("row", "col", None, None),
        P("row", "col"),
    )
    out_specs = (P("col", "row", None), P("col", "row", None))
    return jax.shard_map(
        shards, mesh=mesh, in_specs=in_specs, out_specs=out_specs, check_vma=False
    )
```

```python
import functools

import jax
import jax.numpy as jnp
from jax import lax
from jax.experimental import pallas as pl
from jax.experimental.pallas import tpu as pltpu
from jax.sharding import PartitionSpec as P

ITERS = 3
DIFFUSION = 0.8
RC = ("row", "col")


def split_id(device):
    r, c = divmod(device, 16)
    yh, x = divmod(r, 4)
    yl, q = divmod(c, 8)
    return yh * 2 + yl, x, q // 2, q % 2


def device_id(y, x, z, k):
    return ((y // 2) * 4 + x) * 16 + (y % 2) * 8 + z * 2 + k


def groups_by(key):
    groups = {}
    for device in range(128):
        groups.setdefault(key(*split_id(device)), []).append(device)
    return list(groups.values())


PLANES = groups_by(lambda y, x, z, k: (y, k))
SHEETS = groups_by(lambda y, x, z, k: (x, k))


def shift_y(d):
    pairs = []
    for device in range(128):
        y, x, z, k = split_id(device)
        pairs.append((device, device_id((y + d) % 4, x, z, k)))
    return pairs


SWAP = [(device, device ^ 1) for device in range(128)]


def exchange(send, groups):
    return lax.all_to_all(send, RC, 0, 0, axis_index_groups=groups, tiled=True)


def call(body, limit=16, **kw):
    return pl.pallas_call(
        body, compiler_params=pltpu.CompilerParams(vmem_limit_bytes=limit * 2**20), **kw
    )


def assemble_body(codes, *refs):
    pieces, recv, (hi, lo, share, dense) = refs[:8], refs[8], refs[9:]
    share[...] = recv[:, :64, :]
    dense[...] = jnp.zeros_like(dense)
    y = codes[64]
    for i, ref in enumerate(pieces):
        base = ((y - i // 2) & 3) * 16 + (i % 2) * 8
        for b in range(8):
            code = codes[base + b]

            @pl.when(code >= 0)
            def _(ref=ref, b=b, code=code):
                ro = pl.multiple_of((code >> 3) * 128, 128)
                co = pl.multiple_of((code & 7) * 128, 128)
                dense[pl.ds(ro, 128), pl.ds(co, 128)] += ref[b]

    def narrow(i, carry):
        rows = pl.ds(pl.multiple_of(i * 128, 128), 128)
        value = dense[rows, :]
        top = value.astype(jnp.bfloat16)
        hi[rows, :] = top
        lo[rows, :] = (value - top.astype(jnp.float32)).astype(jnp.bfloat16)
        return carry

    lax.fori_loop(0, 16, narrow, 0)


VMEM = pl.BlockSpec(memory_space=pltpu.VMEM)


def assemble(codes, pieces, recv):
    half = jax.ShapeDtypeStruct((2048, 1024), jnp.bfloat16)
    return call(
        assemble_body,
        limit=24,
        out_shape=(half, half, jax.ShapeDtypeStruct((16, 64, 128), jnp.float32)),
        in_specs=[pl.BlockSpec(memory_space=pltpu.SMEM)] + [VMEM] * 9,
        out_specs=(VMEM,) * 3,
        scratch_shapes=[pltpu.VMEM((2048, 1024), jnp.float32)],
        name="assemble",
    )(codes, *pieces, recv)


def parted(value):
    top = value.astype(jnp.bfloat16)
    return top, (value - top.astype(jnp.float32)).astype(jnp.bfloat16)


def dot(a, b):
    return jnp.dot(a, b, preferred_element_type=jnp.float32)


def chunk(ref, j):
    return ref[:, j * 16 : j * 16 + 16, :].reshape(256, 128)


def part_right(recv, right):
    for s in range(4):
        top, rest = parted(chunk(recv, 4 + s))
        right[pl.ds(s * 256, 256), :128] = top
        right[pl.ds(s * 256, 256), 128:] = rest


def forward(hi, lo, right):
    wide = dot(hi, right[...])
    return wide[:, :128] + wide[:, 128:] + dot(lo, right[:, :128])


def mate_body(recv, hi, lo, out, right):
    part_right(recv, right)
    for i in range(2):
        rows = slice(1024 + i * 512, 1536 + i * 512)
        out[i * 512 : (i + 1) * 512, :] = forward(hi[rows, :], lo[rows, :], right)


def mate(recv, hi, lo):
    return call(
        mate_body,
        out_shape=jax.ShapeDtypeStruct((1024, 128), jnp.float32),
        in_specs=[VMEM] * 3,
        out_specs=VMEM,
        scratch_shapes=[pltpu.VMEM((1024, 256), jnp.bfloat16)],
        name="mate",
    )(recv, hi, lo)


def mirror_body(recv, other, hi, lo, sums, out, scalars, back):
    for i in range(4):
        ref = (recv, other)[i // 2]
        pairs = [parted(chunk(ref, (i % 2) * 2 + c).T) for c in range(2)]
        top = jnp.concatenate([pair[0] for pair in pairs], axis=1)
        rest = jnp.concatenate([pair[1] for pair in pairs], axis=1)
        rows = slice(i * 512, (i + 1) * 512)
        wide = dot(jnp.concatenate([top, rest], axis=0), hi[rows, :])
        part = wide[:128] + wide[128:] + dot(top, lo[rows, :])
        back[...] = part if i == 0 else back[...] + part
    out[...] = back[...].T
    curve = jnp.zeros((8, 128), jnp.float32)
    for s in range(4):
        piece = chunk(recv, 4 + s) * out[s * 256 : (s + 1) * 256]
        curve = curve + jnp.sum(piece.reshape(32, 8, 128), axis=0)
    place = lax.broadcasted_iota(jnp.int32, (8, 128), 0)
    scalars[...] = jnp.where(place == 2, row_sum(curve) * (2 * DIFFUSION), sums[...])


def mirror(recv, other, hi, lo, sums):
    return call(
        mirror_body,
        out_shape=(
            jax.ShapeDtypeStruct((1024, 128), jnp.float32),
            jax.ShapeDtypeStruct((8, 128), jnp.float32),
        ),
        in_specs=[VMEM] * 5,
        out_specs=(VMEM, VMEM),
        scratch_shapes=[pltpu.VMEM((128, 1024), jnp.float32)],
        name="mirror",
    )(recv, other, hi, lo, sums)


def own_body(recv, hi, lo, after, out, right):
    part_right(recv, right)
    for i in range(2):
        rows = slice(i * 512, (i + 1) * 512)
        out[rows, :] = forward(hi[rows, :], lo[rows, :], right)


def own_rows(recv, hi, lo, after):
    return call(
        own_body,
        out_shape=jax.ShapeDtypeStruct((1024, 128), jnp.float32),
        in_specs=[VMEM] * 4,
        out_specs=VMEM,
        scratch_shapes=[pltpu.VMEM((1024, 256), jnp.bfloat16)],
        name="own_rows",
    )(recv, hi, lo, after)


def join_body(ours, theirs, mirrored, mine, mates, out):
    for s in range(4):
        rows = slice(s * 256, (s + 1) * 256)
        part = ours[rows, :] + theirs[rows, :]
        out[:, s * 16 : s * 16 + 16, :] = part.reshape(16, 16, 128)
        out[:, 64 + s * 16 : 80 + s * 16, :] = mirrored[rows, :].reshape(16, 16, 128)
    row = mine[...] + mates[...]
    out[:, 128:136, :] = jnp.broadcast_to(row[None], (16, 8, 128))


def join(ours, theirs, mirrored, mine, mates):
    return call(
        join_body,
        out_shape=jax.ShapeDtypeStruct((16, 136, 128), jnp.float32),
        in_specs=[VMEM] * 5,
        out_specs=VMEM,
        name="join",
    )(ours, theirs, mirrored, mine, mates)


def multiply(recv, share, sums, hi, lo):
    other = lax.ppermute(share, RC, SWAP)
    theirs = lax.ppermute(mate(recv, hi, lo), RC, SWAP)
    mirrored, mine = mirror(recv, other, hi, lo, sums)
    mates = lax.ppermute(mine, RC, SWAP)
    ours = own_rows(recv, hi, lo, mine)
    return join(ours, theirs, mirrored, mine, mates)


def spread(field, send):
    for s in range(4):
        for g in range(4):
            piece = field(s, g)
            for other in range(4):
                send[g * 4 + other, s * 16 : s * 16 + 16, :] = piece
                send[other * 4 + g, 64 + s * 16 : 80 + s * 16, :] = piece


def row_sum(value):
    return jnp.sum(value, axis=0, keepdims=True)


def rows_of(*rows):
    place = lax.broadcasted_iota(jnp.int32, (8, 128), 0)
    out = jnp.zeros((8, 128), jnp.float32)
    for i, row in enumerate(rows):
        out = jnp.where(place == i, row, out)
    return out


def start_body(recv, send, sums):
    square = jnp.zeros((16, 128), jnp.float32)
    for i in range(16):
        piece = recv[i, :16]
        square = square + piece * piece
    spread(lambda s, g: recv[s * 4 + g, :16], send)
    sums[...] = rows_of(row_sum(square))


def start(recv):
    return call(
        start_body,
        out_shape=(
            jax.ShapeDtypeStruct((16, 128, 128), jnp.float32),
            jax.ShapeDtypeStruct((8, 128), jnp.float32),
        ),
        name="start",
    )(recv)


def update_body(step, *refs):
    if step == 0:
        recv, residual = refs[:2]
        outs = refs[2:]
    else:
        recv, residual, direction, image, ranking, last = refs[:6]
        outs = refs[6:]
    total = jnp.zeros((8, 128), jnp.float32)
    for i in range(16):
        total = total + recv[i, 128:136]
    now = total[0:1]
    curve = now - total[2:3]
    if step > 0:
        beta = now / last[0:1]
        curve = curve + 2.0 * beta * total[1:2] + beta * beta * last[1:2]
    alpha = now / curve
    final = step + 1 == ITERS
    square = jnp.zeros((16, 128), jnp.float32)
    cross = jnp.zeros((16, 128), jnp.float32)
    for s in range(4):
        for g in range(4):
            acc = jnp.zeros((16, 128), jnp.float32)
            for other in range(4):
                acc = acc + recv[g * 4 + other, s * 16 : s * 16 + 16]
                acc = acc + recv[other * 4 + g, 64 + s * 16 : 80 + s * 16]
            i = s * 4 + g
            rest = residual[i, :16]
            aim = rest
            made = rest - DIFFUSION * acc
            if step > 0:
                aim = aim + beta * direction[i]
                made = made + beta * image[i]
            ranked = alpha * aim
            if step > 0:
                ranked = ranked + ranking[i]
            rest = rest - alpha * made
            if final:
                outs[0][i, 0] = ranked
                outs[0][i, 1] = rest
            else:
                send, new_residual, new_direction, new_image, new_ranking = outs[:5]
                new_residual[i] = rest
                new_direction[i] = aim
                new_image[i] = made
                new_ranking[i] = ranked
                square = square + rest * rest
                cross = cross + rest * made
    if not final:
        spread(lambda s, g: new_residual[s * 4 + g], send)
        outs[5][...] = rows_of(now, curve)
        outs[6][...] = rows_of(row_sum(square), row_sum(cross))


def update(step, *operands):
    field = jax.ShapeDtypeStruct((16, 16, 128), jnp.float32)
    small = jax.ShapeDtypeStruct((8, 128), jnp.float32)
    if step + 1 == ITERS:
        shapes = [jax.ShapeDtypeStruct((16, 2, 16, 128), jnp.float32)]
    else:
        send = jax.ShapeDtypeStruct((16, 128, 128), jnp.float32)
        shapes = [send, field, field, field, field, small, small]
    return call(
        functools.partial(update_body, step), out_shape=shapes, name="update"
    )(*operands)


def deliver_body(recv, *outs):
    for y in range(4):
        for z in range(4):
            for which, out in enumerate(outs):
                out[0, z * 16 : z * 16 + 16, y * 128 : y * 128 + 128] = recv[y * 4 + z, which]


def deliver(recv):
    out = jax.ShapeDtypeStruct((1, 64, 512), jnp.float32)
    return call(deliver_body, out_shape=(out, out), name="deliver")(recv)


def shards(right_side, affinity_blocks, block_coords, block_counts):
    r = lax.axis_index("row")
    c = lax.axis_index("col")
    yh, yl, z, k = r // 4, c // 8, (c // 2) % 4, c % 2
    own0 = affinity_blocks[0, 0]
    own1 = affinity_blocks[1, 0]
    left0 = lax.ppermute(own0, RC, shift_y(1))
    right1 = lax.ppermute(own1, RC, shift_y(3))

    br = block_coords[:, 0, :, 0]
    bc = block_coords[:, 0, :, 1]
    par = jnp.arange(2, dtype=jnp.int32)[:, None] ^ k
    row128 = par * 8 + ((br // 2) * 2 + yh) * 2 + br % 2
    col128 = ((bc // 2) * 2 + yl) * 2 + bc % 2
    live = jnp.arange(8, dtype=jnp.int32)[None, :] < block_counts
    code = jnp.where(live, row128 * 8 + col128, -1).astype(jnp.float32)
    meta = jnp.pad(code.reshape(1, 16), ((0, 7), (0, 112)))

    send = right_side.reshape(4, 16, 4, 128).transpose(2, 0, 1, 3).reshape(16, 16, 128)
    send = jnp.concatenate([send, jnp.broadcast_to(meta[None], (16, 8, 128))], axis=1)
    recv = exchange(send, SHEETS)
    codes = lax.dynamic_slice(recv.reshape(4, 4, 24, 128), (0, z, 16, 0), (4, 1, 1, 16))
    codes = jnp.concatenate(
        [codes.reshape(64).astype(jnp.int32), (yh * 2 + yl)[None].astype(jnp.int32)]
    )

    send, sums = start(recv)
    state = (recv,)
    send, left0, right1 = lax.optimization_barrier((send, left0, right1))
    later0, later1, recv = lax.optimization_barrier((own0, own1, recv))
    far0 = lax.ppermute(left0, RC, shift_y(1))
    far1 = lax.ppermute(right1, RC, shift_y(3))
    left1 = lax.ppermute(later1, RC, shift_y(1))
    right0 = lax.ppermute(later0, RC, shift_y(3))
    got = exchange(send, PLANES)
    pieces = (own0, own1, left0, left1, far0, far1, right0, right1)
    hi, lo, share = assemble(codes, pieces, got)
    for step in range(ITERS):
        if step:
            got = share = exchange(send, PLANES)
        products = exchange(multiply(got, share, sums, hi, lo), PLANES)
        made = update(step, products, *state)
        if step + 1 < ITERS:
            send, sums = made[0], made[6]
            state = made[1:6]
    done = exchange(made[0], SHEETS)
    return tuple(deliver(done))


def solution(mesh):
    in_specs = (
        P("col", "row", None),
        P("row", "col", None, None, None),
        P("row", "col", None, None),
        P("row", "col"),
    )
    out_specs = (P("col", "row", None), P("col", "row", None))
    return jax.shard_map(
        shards, mesh=mesh, in_specs=in_specs, out_specs=out_specs, check_vma=False
    )
```

```python
import functools

import jax
import jax.numpy as jnp
from jax import lax
from jax.experimental import pallas as pl
from jax.experimental.pallas import tpu as pltpu
from jax.sharding import PartitionSpec as P

ITERS = 3
DIFFUSION = 0.8
RC = ("row", "col")


def split_id(device):
    r, c = divmod(device, 16)
    yh, x = divmod(r, 4)
    yl, q = divmod(c, 8)
    return yh * 2 + yl, x, q // 2, q % 2


def device_id(y, x, z, k):
    return ((y // 2) * 4 + x) * 16 + (y % 2) * 8 + z * 2 + k


def groups_by(key):
    groups = {}
    for device in range(128):
        groups.setdefault(key(*split_id(device)), []).append(device)
    return list(groups.values())


PLANES = groups_by(lambda y, x, z, k: (y, k))
SHEETS = groups_by(lambda y, x, z, k: (x, k))


def shift_y(d):
    pairs = []
    for device in range(128):
        y, x, z, k = split_id(device)
        pairs.append((device, device_id((y + d) % 4, x, z, k)))
    return pairs


SWAP = [(device, device ^ 1) for device in range(128)]


def exchange(send, groups):
    return lax.all_to_all(send, RC, 0, 0, axis_index_groups=groups, tiled=True)


def call(body, limit=16, **kw):
    return pl.pallas_call(
        body, compiler_params=pltpu.CompilerParams(vmem_limit_bytes=limit * 2**20), **kw
    )


def assemble_body(codes, *refs):
    own0, own1, left0, right1, wave, back, recv, hi, lo, share, dense = refs
    pieces = (
        (own0, 0), (own1, 0), (left0, 0), (wave, 8), (wave, 0), (back, 0), (back, 8), (right1, 0)
    )
    share[...] = recv[:, :64, :]
    dense[...] = jnp.zeros_like(dense)
    y = codes[64]
    for i, (ref, first) in enumerate(pieces):
        base = ((y - i // 2) & 3) * 16 + (i % 2) * 8
        for b in range(8):
            code = codes[base + b]

            @pl.when(code >= 0)
            def _(ref=ref, b=first + b, code=code):
                ro = pl.multiple_of((code >> 3) * 128, 128)
                co = pl.multiple_of((code & 7) * 128, 128)
                dense[pl.ds(ro, 128), pl.ds(co, 128)] += ref[b]

    def narrow(i, carry):
        rows = pl.ds(pl.multiple_of(i * 128, 128), 128)
        value = dense[rows, :]
        top = value.astype(jnp.bfloat16)
        hi[rows, :] = top
        lo[rows, :] = (value - top.astype(jnp.float32)).astype(jnp.bfloat16)
        return carry

    lax.fori_loop(0, 16, narrow, 0)


VMEM = pl.BlockSpec(memory_space=pltpu.VMEM)


def assemble(codes, pieces, recv):
    half = jax.ShapeDtypeStruct((2048, 1024), jnp.bfloat16)
    return call(
        assemble_body,
        limit=24,
        out_shape=(half, half, jax.ShapeDtypeStruct((16, 64, 128), jnp.float32)),
        in_specs=[pl.BlockSpec(memory_space=pltpu.SMEM)] + [VMEM] * 7,
        out_specs=(VMEM,) * 3,
        scratch_shapes=[pltpu.VMEM((2048, 1024), jnp.float32)],
        name="assemble",
    )(codes, *pieces, recv)


def parted(value):
    top = value.astype(jnp.bfloat16)
    return top, (value - top.astype(jnp.float32)).astype(jnp.bfloat16)


def dot(a, b):
    return jnp.dot(a, b, preferred_element_type=jnp.float32)


def chunk(ref, j):
    return ref[:, j * 16 : j * 16 + 16, :].reshape(256, 128)


def part_right(recv, right):
    for s in range(4):
        top, rest = parted(chunk(recv, 4 + s))
        right[pl.ds(s * 256, 256), :128] = top
        right[pl.ds(s * 256, 256), 128:] = rest


def forward(hi, lo, right):
    wide = dot(hi, right[...])
    return wide[:, :128] + wide[:, 128:] + dot(lo, right[:, :128])


def mate_body(recv, hi, lo, out, right):
    part_right(recv, right)
    for i in range(2):
        rows = slice(1024 + i * 512, 1536 + i * 512)
        out[i * 512 : (i + 1) * 512, :] = forward(hi[rows, :], lo[rows, :], right)


def mate(recv, hi, lo):
    return call(
        mate_body,
        out_shape=jax.ShapeDtypeStruct((1024, 128), jnp.float32),
        in_specs=[VMEM] * 3,
        out_specs=VMEM,
        scratch_shapes=[pltpu.VMEM((1024, 256), jnp.bfloat16)],
        name="mate",
    )(recv, hi, lo)


def mirror_body(recv, other, hi, lo, sums, out, scalars, back):
    for i in range(4):
        ref = (recv, other)[i // 2]
        pairs = [parted(chunk(ref, (i % 2) * 2 + c).T) for c in range(2)]
        top = jnp.concatenate([pair[0] for pair in pairs], axis=1)
        rest = jnp.concatenate([pair[1] for pair in pairs], axis=1)
        rows = slice(i * 512, (i + 1) * 512)
        wide = dot(jnp.concatenate([top, rest], axis=0), hi[rows, :])
        part = wide[:128] + wide[128:] + dot(top, lo[rows, :])
        back[...] = part if i == 0 else back[...] + part
    out[...] = back[...].T
    curve = jnp.zeros((8, 128), jnp.float32)
    for s in range(4):
        piece = chunk(recv, 4 + s) * out[s * 256 : (s + 1) * 256]
        curve = curve + jnp.sum(piece.reshape(32, 8, 128), axis=0)
    place = lax.broadcasted_iota(jnp.int32, (8, 128), 0)
    scalars[...] = jnp.where(place == 2, row_sum(curve) * (2 * DIFFUSION), sums[...])


def mirror(recv, other, hi, lo, sums):
    return call(
        mirror_body,
        out_shape=(
            jax.ShapeDtypeStruct((1024, 128), jnp.float32),
            jax.ShapeDtypeStruct((8, 128), jnp.float32),
        ),
        in_specs=[VMEM] * 5,
        out_specs=(VMEM, VMEM),
        scratch_shapes=[pltpu.VMEM((128, 1024), jnp.float32)],
        name="mirror",
    )(recv, other, hi, lo, sums)


def own_body(recv, hi, lo, after, out, right):
    part_right(recv, right)
    for i in range(2):
        rows = slice(i * 512, (i + 1) * 512)
        out[rows, :] = forward(hi[rows, :], lo[rows, :], right)


def own_rows(recv, hi, lo, after):
    return call(
        own_body,
        out_shape=jax.ShapeDtypeStruct((1024, 128), jnp.float32),
        in_specs=[VMEM] * 4,
        out_specs=VMEM,
        scratch_shapes=[pltpu.VMEM((1024, 256), jnp.bfloat16)],
        name="own_rows",
    )(recv, hi, lo, after)


def join_body(ours, theirs, mirrored, mine, mates, out):
    for s in range(4):
        rows = slice(s * 256, (s + 1) * 256)
        part = ours[rows, :] + theirs[rows, :]
        out[:, s * 16 : s * 16 + 16, :] = part.reshape(16, 16, 128)
        out[:, 64 + s * 16 : 80 + s * 16, :] = mirrored[rows, :].reshape(16, 16, 128)
    row = mine[...] + mates[...]
    out[:, 128:136, :] = jnp.broadcast_to(row[None], (16, 8, 128))


def join(ours, theirs, mirrored, mine, mates):
    return call(
        join_body,
        out_shape=jax.ShapeDtypeStruct((16, 136, 128), jnp.float32),
        in_specs=[VMEM] * 5,
        out_specs=VMEM,
        name="join",
    )(ours, theirs, mirrored, mine, mates)


def multiply(recv, share, sums, hi, lo):
    other = lax.ppermute(share, RC, SWAP)
    theirs = lax.ppermute(mate(recv, hi, lo), RC, SWAP)
    mirrored, mine = mirror(recv, other, hi, lo, sums)
    mates = lax.ppermute(mine, RC, SWAP)
    ours = own_rows(recv, hi, lo, mine)
    return join(ours, theirs, mirrored, mine, mates)


def spread(field, send):
    for s in range(4):
        for g in range(4):
            piece = field(s, g)
            for other in range(4):
                send[g * 4 + other, s * 16 : s * 16 + 16, :] = piece
                send[other * 4 + g, 64 + s * 16 : 80 + s * 16, :] = piece


def row_sum(value):
    return jnp.sum(value, axis=0, keepdims=True)


def rows_of(*rows):
    place = lax.broadcasted_iota(jnp.int32, (8, 128), 0)
    out = jnp.zeros((8, 128), jnp.float32)
    for i, row in enumerate(rows):
        out = jnp.where(place == i, row, out)
    return out


def start_body(recv, send, sums):
    square = jnp.zeros((16, 128), jnp.float32)
    for i in range(16):
        piece = recv[i, :16]
        square = square + piece * piece
    spread(lambda s, g: recv[s * 4 + g, :16], send)
    sums[...] = rows_of(row_sum(square))


def start(recv):
    return call(
        start_body,
        out_shape=(
            jax.ShapeDtypeStruct((16, 128, 128), jnp.float32),
            jax.ShapeDtypeStruct((8, 128), jnp.float32),
        ),
        name="start",
    )(recv)


def update_body(step, *refs):
    if step == 0:
        recv, residual = refs[:2]
        outs = refs[2:]
    else:
        recv, residual, direction, image, ranking, last = refs[:6]
        outs = refs[6:]
    total = jnp.zeros((8, 128), jnp.float32)
    for i in range(16):
        total = total + recv[i, 128:136]
    now = total[0:1]
    curve = now - total[2:3]
    if step > 0:
        beta = now / last[0:1]
        curve = curve + 2.0 * beta * total[1:2] + beta * beta * last[1:2]
    alpha = now / curve
    final = step + 1 == ITERS
    square = jnp.zeros((16, 128), jnp.float32)
    cross = jnp.zeros((16, 128), jnp.float32)
    for s in range(4):
        for g in range(4):
            acc = jnp.zeros((16, 128), jnp.float32)
            for other in range(4):
                acc = acc + recv[g * 4 + other, s * 16 : s * 16 + 16]
                acc = acc + recv[other * 4 + g, 64 + s * 16 : 80 + s * 16]
            i = s * 4 + g
            rest = residual[i, :16]
            aim = rest
            made = rest - DIFFUSION * acc
            if step > 0:
                aim = aim + beta * direction[i]
                made = made + beta * image[i]
            ranked = alpha * aim
            if step > 0:
                ranked = ranked + ranking[i]
            rest = rest - alpha * made
            if final:
                outs[0][i, 0] = ranked
                outs[0][i, 1] = rest
            else:
                send, new_residual, new_direction, new_image, new_ranking = outs[:5]
                new_residual[i] = rest
                new_direction[i] = aim
                new_image[i] = made
                new_ranking[i] = ranked
                square = square + rest * rest
                cross = cross + rest * made
    if not final:
        spread(lambda s, g: new_residual[s * 4 + g], send)
        outs[5][...] = rows_of(now, curve)
        outs[6][...] = rows_of(row_sum(square), row_sum(cross))


def update(step, *operands):
    field = jax.ShapeDtypeStruct((16, 16, 128), jnp.float32)
    small = jax.ShapeDtypeStruct((8, 128), jnp.float32)
    if step + 1 == ITERS:
        shapes = [jax.ShapeDtypeStruct((16, 2, 16, 128), jnp.float32)]
    else:
        send = jax.ShapeDtypeStruct((16, 128, 128), jnp.float32)
        shapes = [send, field, field, field, field, small, small]
    return call(
        functools.partial(update_body, step), out_shape=shapes, name="update"
    )(*operands)


def deliver_body(recv, *outs):
    for y in range(4):
        for z in range(4):
            for which, out in enumerate(outs):
                out[0, z * 16 : z * 16 + 16, y * 128 : y * 128 + 128] = recv[y * 4 + z, which]


def deliver(recv):
    out = jax.ShapeDtypeStruct((1, 64, 512), jnp.float32)
    return call(deliver_body, out_shape=(out, out), name="deliver")(recv)


def shards(right_side, affinity_blocks, block_coords, block_counts):
    r = lax.axis_index("row")
    c = lax.axis_index("col")
    yh, yl, z, k = r // 4, c // 8, (c // 2) % 4, c % 2
    own0 = affinity_blocks[0, 0]
    own1 = affinity_blocks[1, 0]
    left0 = lax.ppermute(own0, RC, shift_y(1))
    right1 = lax.ppermute(own1, RC, shift_y(3))

    br = block_coords[:, 0, :, 0]
    bc = block_coords[:, 0, :, 1]
    par = jnp.arange(2, dtype=jnp.int32)[:, None] ^ k
    row128 = par * 8 + ((br // 2) * 2 + yh) * 2 + br % 2
    col128 = ((bc // 2) * 2 + yl) * 2 + bc % 2
    live = jnp.arange(8, dtype=jnp.int32)[None, :] < block_counts
    code = jnp.where(live, row128 * 8 + col128, -1).astype(jnp.float32)
    meta = jnp.pad(code.reshape(1, 16), ((0, 7), (0, 112)))

    send = right_side.reshape(4, 16, 4, 128).transpose(2, 0, 1, 3).reshape(16, 16, 128)
    send = jnp.concatenate([send, jnp.broadcast_to(meta[None], (16, 8, 128))], axis=1)
    recv = exchange(send, SHEETS)
    codes = lax.dynamic_slice(recv.reshape(4, 4, 24, 128), (0, z, 16, 0), (4, 1, 1, 16))
    codes = jnp.concatenate(
        [codes.reshape(64).astype(jnp.int32), (yh * 2 + yl)[None].astype(jnp.int32)]
    )

    send, sums = start(recv)
    state = (recv,)
    send, left0, right1 = lax.optimization_barrier((send, left0, right1))
    wave, back, recv = lax.optimization_barrier(
        (jnp.concatenate([left0, own1]), jnp.concatenate([right1, own0]), recv)
    )
    wave = lax.ppermute(wave, RC, shift_y(1))
    back = lax.ppermute(back, RC, shift_y(3))
    got = exchange(send, PLANES)
    pieces = (own0, own1, left0, right1, wave, back)
    hi, lo, share = assemble(codes, pieces, got)
    for step in range(ITERS):
        if step:
            got = share = exchange(send, PLANES)
        products = exchange(multiply(got, share, sums, hi, lo), PLANES)
        made = update(step, products, *state)
        if step + 1 < ITERS:
            send, sums = made[0], made[6]
            state = made[1:6]
    done = exchange(made[0], SHEETS)
    return tuple(deliver(done))


def solution(mesh):
    in_specs = (
        P("col", "row", None),
        P("row", "col", None, None, None),
        P("row", "col", None, None),
        P("row", "col"),
    )
    out_specs = (P("col", "row", None), P("col", "row", None))
    return jax.shard_map(
        shards, mesh=mesh, in_specs=in_specs, out_specs=out_specs, check_vma=False
    )
```

```python
import functools

import jax
import jax.numpy as jnp
from jax import lax
from jax.experimental import pallas as pl
from jax.experimental.pallas import tpu as pltpu
from jax.sharding import PartitionSpec as P

ITERS = 3
DIFFUSION = 0.8
RC = ("row", "col")


def split_id(device):
    r, c = divmod(device, 16)
    yh, x = divmod(r, 4)
    yl, q = divmod(c, 8)
    return yh * 2 + yl, x, q // 2, q % 2


def device_id(y, x, z, k):
    return ((y // 2) * 4 + x) * 16 + (y % 2) * 8 + z * 2 + k


def groups_by(key):
    groups = {}
    for device in range(128):
        groups.setdefault(key(*split_id(device)), []).append(device)
    return list(groups.values())


PLANES = groups_by(lambda y, x, z, k: (y, k))
SHEETS = groups_by(lambda y, x, z, k: (x, k))


def shift_y(d):
    pairs = []
    for device in range(128):
        y, x, z, k = split_id(device)
        pairs.append((device, device_id((y + d) % 4, x, z, k)))
    return pairs


SWAP = [(device, device ^ 1) for device in range(128)]


def exchange(send, groups):
    return lax.all_to_all(send, RC, 0, 0, axis_index_groups=groups, tiled=True)


def call(body, limit=16, **kw):
    return pl.pallas_call(
        body, compiler_params=pltpu.CompilerParams(vmem_limit_bytes=limit * 2**20), **kw
    )


def assemble_body(codes, *refs):
    own0, own1, left0, right1, wave_in, back_in, recv, hi, lo, share, dense, wave, back, sems = refs
    copies = (
        pltpu.make_async_copy(wave_in, wave, sems.at[0]),
        pltpu.make_async_copy(back_in, back, sems.at[1]),
    )
    for copy in copies:
        copy.start()
    pieces = (
        (own0, 0, 0, 0), (own1, 0, 0, 1), (left0, 0, 1, 0), (right1, 0, 3, 1),
        (wave, 8, 1, 1), (wave, 0, 2, 0), (back, 0, 2, 1), (back, 8, 3, 0),
    )
    share[...] = recv[:, :64, :]
    dense[...] = jnp.zeros_like(dense)
    y = codes[64]
    for i, (ref, first, d, h) in enumerate(pieces):
        base = ((y - d) & 3) * 16 + h * 8
        if i == 4:
            for copy in copies:
                copy.wait()
        for b in range(8):
            code = codes[base + b]

            @pl.when(code >= 0)
            def _(ref=ref, b=first + b, code=code):
                ro = pl.multiple_of((code >> 3) * 128, 128)
                co = pl.multiple_of((code & 7) * 128, 128)
                dense[pl.ds(ro, 128), pl.ds(co, 128)] += ref[b]

    def narrow(i, carry):
        rows = pl.ds(pl.multiple_of(i * 128, 128), 128)
        value = dense[rows, :]
        top = value.astype(jnp.bfloat16)
        hi[rows, :] = top
        lo[rows, :] = (value - top.astype(jnp.float32)).astype(jnp.bfloat16)
        return carry

    lax.fori_loop(0, 16, narrow, 0)


VMEM = pl.BlockSpec(memory_space=pltpu.VMEM)
HBM = pl.BlockSpec(memory_space=pltpu.HBM)


def assemble(codes, pieces, recv):
    half = jax.ShapeDtypeStruct((2048, 1024), jnp.bfloat16)
    return call(
        assemble_body,
        limit=24,
        out_shape=(half, half, jax.ShapeDtypeStruct((16, 64, 128), jnp.float32)),
        in_specs=[pl.BlockSpec(memory_space=pltpu.SMEM)] + [VMEM] * 4 + [HBM] * 2 + [VMEM],
        out_specs=(VMEM,) * 3,
        scratch_shapes=[pltpu.VMEM((2048, 1024), jnp.float32)]
        + [pltpu.VMEM((16, 128, 128), jnp.float32)] * 2
        + [pltpu.SemaphoreType.DMA((2,))],
        name="assemble",
    )(codes, *pieces, recv)


def parted(value):
    top = value.astype(jnp.bfloat16)
    return top, (value - top.astype(jnp.float32)).astype(jnp.bfloat16)


def dot(a, b):
    return jnp.dot(a, b, preferred_element_type=jnp.float32)


def chunk(ref, j):
    return ref[:, j * 16 : j * 16 + 16, :].reshape(256, 128)


def part_right(recv, right):
    for s in range(4):
        top, rest = parted(chunk(recv, 4 + s))
        right[pl.ds(s * 256, 256), :128] = top
        right[pl.ds(s * 256, 256), 128:] = rest


def forward(hi, lo, right):
    wide = dot(hi, right[...])
    return wide[:, :128] + wide[:, 128:] + dot(lo, right[:, :128])


def mate_body(recv, hi, lo, out, right):
    part_right(recv, right)
    for i in range(2):
        rows = slice(1024 + i * 512, 1536 + i * 512)
        out[i * 512 : (i + 1) * 512, :] = forward(hi[rows, :], lo[rows, :], right)


def mate(recv, hi, lo):
    return call(
        mate_body,
        out_shape=jax.ShapeDtypeStruct((1024, 128), jnp.float32),
        in_specs=[VMEM] * 3,
        out_specs=VMEM,
        scratch_shapes=[pltpu.VMEM((1024, 256), jnp.bfloat16)],
        name="mate",
    )(recv, hi, lo)


def mirror_body(recv, other, hi, lo, sums, out, scalars, back):
    for i in range(4):
        ref = (recv, other)[i // 2]
        pairs = [parted(chunk(ref, (i % 2) * 2 + c).T) for c in range(2)]
        top = jnp.concatenate([pair[0] for pair in pairs], axis=1)
        rest = jnp.concatenate([pair[1] for pair in pairs], axis=1)
        rows = slice(i * 512, (i + 1) * 512)
        wide = dot(jnp.concatenate([top, rest], axis=0), hi[rows, :])
        part = wide[:128] + wide[128:] + dot(top, lo[rows, :])
        back[...] = part if i == 0 else back[...] + part
    out[...] = back[...].T
    curve = jnp.zeros((8, 128), jnp.float32)
    for s in range(4):
        piece = chunk(recv, 4 + s) * out[s * 256 : (s + 1) * 256]
        curve = curve + jnp.sum(piece.reshape(32, 8, 128), axis=0)
    place = lax.broadcasted_iota(jnp.int32, (8, 128), 0)
    scalars[...] = jnp.where(place == 2, row_sum(curve) * (2 * DIFFUSION), sums[...])


def mirror(recv, other, hi, lo, sums):
    return call(
        mirror_body,
        out_shape=(
            jax.ShapeDtypeStruct((1024, 128), jnp.float32),
            jax.ShapeDtypeStruct((8, 128), jnp.float32),
        ),
        in_specs=[VMEM] * 5,
        out_specs=(VMEM, VMEM),
        scratch_shapes=[pltpu.VMEM((128, 1024), jnp.float32)],
        name="mirror",
    )(recv, other, hi, lo, sums)


def own_body(recv, hi, lo, after, out, right):
    part_right(recv, right)
    for i in range(2):
        rows = slice(i * 512, (i + 1) * 512)
        out[rows, :] = forward(hi[rows, :], lo[rows, :], right)


def own_rows(recv, hi, lo, after):
    return call(
        own_body,
        out_shape=jax.ShapeDtypeStruct((1024, 128), jnp.float32),
        in_specs=[VMEM] * 4,
        out_specs=VMEM,
        scratch_shapes=[pltpu.VMEM((1024, 256), jnp.bfloat16)],
        name="own_rows",
    )(recv, hi, lo, after)


def join_body(ours, theirs, mirrored, mine, mates, out):
    for s in range(4):
        rows = slice(s * 256, (s + 1) * 256)
        part = ours[rows, :] + theirs[rows, :]
        out[:, s * 16 : s * 16 + 16, :] = part.reshape(16, 16, 128)
        out[:, 64 + s * 16 : 80 + s * 16, :] = mirrored[rows, :].reshape(16, 16, 128)
    row = mine[...] + mates[...]
    out[:, 128:136, :] = jnp.broadcast_to(row[None], (16, 8, 128))


def join(ours, theirs, mirrored, mine, mates):
    return call(
        join_body,
        out_shape=jax.ShapeDtypeStruct((16, 136, 128), jnp.float32),
        in_specs=[VMEM] * 5,
        out_specs=VMEM,
        name="join",
    )(ours, theirs, mirrored, mine, mates)


def multiply(recv, share, sums, hi, lo):
    other = lax.ppermute(share, RC, SWAP)
    theirs = lax.ppermute(mate(recv, hi, lo), RC, SWAP)
    mirrored, mine = mirror(recv, other, hi, lo, sums)
    mates = lax.ppermute(mine, RC, SWAP)
    ours = own_rows(recv, hi, lo, mine)
    return join(ours, theirs, mirrored, mine, mates)


def spread(field, send):
    for s in range(4):
        for g in range(4):
            piece = field(s, g)
            for other in range(4):
                send[g * 4 + other, s * 16 : s * 16 + 16, :] = piece
                send[other * 4 + g, 64 + s * 16 : 80 + s * 16, :] = piece


def row_sum(value):
    return jnp.sum(value, axis=0, keepdims=True)


def rows_of(*rows):
    place = lax.broadcasted_iota(jnp.int32, (8, 128), 0)
    out = jnp.zeros((8, 128), jnp.float32)
    for i, row in enumerate(rows):
        out = jnp.where(place == i, row, out)
    return out


def start_body(recv, left0, own1, right1, own0, send, sums, wave, back, work, sems):
    pieces = ((left0, wave, 0), (own1, wave, 8), (right1, back, 0), (own0, back, 8))
    copies = [
        pltpu.make_async_copy(src, dst.at[pl.ds(first, 8)], sems.at[i])
        for i, (src, dst, first) in enumerate(pieces)
    ]
    for copy in copies:
        copy.start()
    spread(lambda s, g: recv[s * 4 + g, :16], work)
    copies.append(pltpu.make_async_copy(work, send, sems.at[4]))
    copies[-1].start()
    square = jnp.zeros((16, 128), jnp.float32)
    for i in range(16):
        piece = recv[i, :16]
        square = square + piece * piece
    sums[...] = rows_of(row_sum(square))
    for copy in copies:
        copy.wait()


def start(*operands):
    big = jax.ShapeDtypeStruct((16, 128, 128), jnp.float32)
    small = jax.ShapeDtypeStruct((8, 128), jnp.float32)
    return call(
        start_body,
        out_shape=(big, small, big, big),
        in_specs=[VMEM] * 5,
        out_specs=(HBM, VMEM, HBM, HBM),
        scratch_shapes=[
            pltpu.VMEM((16, 128, 128), jnp.float32),
            pltpu.SemaphoreType.DMA((5,)),
        ],
        name="start",
    )(*operands)


def update_body(step, *refs):
    if step == 0:
        recv, residual = refs[:2]
        outs = refs[2:]
    else:
        recv, residual, direction, image, ranking, last = refs[:6]
        outs = refs[6:]
    total = jnp.zeros((8, 128), jnp.float32)
    for i in range(16):
        total = total + recv[i, 128:136]
    now = total[0:1]
    curve = now - total[2:3]
    if step > 0:
        beta = now / last[0:1]
        curve = curve + 2.0 * beta * total[1:2] + beta * beta * last[1:2]
    alpha = now / curve
    final = step + 1 == ITERS
    square = jnp.zeros((16, 128), jnp.float32)
    cross = jnp.zeros((16, 128), jnp.float32)
    for s in range(4):
        for g in range(4):
            acc = jnp.zeros((16, 128), jnp.float32)
            for other in range(4):
                acc = acc + recv[g * 4 + other, s * 16 : s * 16 + 16]
                acc = acc + recv[other * 4 + g, 64 + s * 16 : 80 + s * 16]
            i = s * 4 + g
            rest = residual[i, :16]
            aim = rest
            made = rest - DIFFUSION * acc
            if step > 0:
                aim = aim + beta * direction[i]
                made = made + beta * image[i]
            ranked = alpha * aim
            if step > 0:
                ranked = ranked + ranking[i]
            rest = rest - alpha * made
            if final:
                outs[0][i, 0] = ranked
                outs[0][i, 1] = rest
            else:
                send, new_residual, new_direction, new_image, new_ranking = outs[:5]
                new_residual[i] = rest
                new_direction[i] = aim
                new_image[i] = made
                new_ranking[i] = ranked
                square = square + rest * rest
                cross = cross + rest * made
    if not final:
        spread(lambda s, g: new_residual[s * 4 + g], send)
        outs[5][...] = rows_of(now, curve)
        outs[6][...] = rows_of(row_sum(square), row_sum(cross))


def update(step, *operands):
    field = jax.ShapeDtypeStruct((16, 16, 128), jnp.float32)
    small = jax.ShapeDtypeStruct((8, 128), jnp.float32)
    if step + 1 == ITERS:
        shapes = [jax.ShapeDtypeStruct((16, 2, 16, 128), jnp.float32)]
    else:
        send = jax.ShapeDtypeStruct((16, 128, 128), jnp.float32)
        shapes = [send, field, field, field, field, small, small]
    return call(
        functools.partial(update_body, step), out_shape=shapes, name="update"
    )(*operands)


def deliver_body(recv, *outs):
    for y in range(4):
        for z in range(4):
            for which, out in enumerate(outs):
                out[0, z * 16 : z * 16 + 16, y * 128 : y * 128 + 128] = recv[y * 4 + z, which]


def deliver(recv):
    out = jax.ShapeDtypeStruct((1, 64, 512), jnp.float32)
    return call(deliver_body, out_shape=(out, out), name="deliver")(recv)


def shards(right_side, affinity_blocks, block_coords, block_counts):
    r = lax.axis_index("row")
    c = lax.axis_index("col")
    yh, yl, z, k = r // 4, c // 8, (c // 2) % 4, c % 2
    own0 = affinity_blocks[0, 0]
    own1 = affinity_blocks[1, 0]
    left0 = lax.ppermute(own0, RC, shift_y(1))
    right1 = lax.ppermute(own1, RC, shift_y(3))

    br = block_coords[:, 0, :, 0]
    bc = block_coords[:, 0, :, 1]
    par = jnp.arange(2, dtype=jnp.int32)[:, None] ^ k
    row128 = par * 8 + ((br // 2) * 2 + yh) * 2 + br % 2
    col128 = ((bc // 2) * 2 + yl) * 2 + bc % 2
    live = jnp.arange(8, dtype=jnp.int32)[None, :] < block_counts
    code = jnp.where(live, row128 * 8 + col128, -1).astype(jnp.float32)
    meta = jnp.pad(code.reshape(1, 16), ((0, 7), (0, 112)))

    send = right_side.reshape(4, 16, 4, 128).transpose(2, 0, 1, 3).reshape(16, 16, 128)
    send = jnp.concatenate([send, jnp.broadcast_to(meta[None], (16, 8, 128))], axis=1)
    recv = exchange(send, SHEETS)
    codes = lax.dynamic_slice(recv.reshape(4, 4, 24, 128), (0, z, 16, 0), (4, 1, 1, 16))
    codes = jnp.concatenate(
        [codes.reshape(64).astype(jnp.int32), (yh * 2 + yl)[None].astype(jnp.int32)]
    )

    send, sums, wave, back = start(recv, left0, own1, right1, own0)
    state = (recv,)
    wave = lax.ppermute(wave, RC, shift_y(1))
    back = lax.ppermute(back, RC, shift_y(3))
    got = exchange(send, PLANES)
    pieces = (own0, own1, left0, right1, wave, back)
    hi, lo, share = assemble(codes, pieces, got)
    for step in range(ITERS):
        if step:
            got = share = exchange(send, PLANES)
        products = exchange(multiply(got, share, sums, hi, lo), PLANES)
        made = update(step, products, *state)
        if step + 1 < ITERS:
            send, sums = made[0], made[6]
            state = made[1:6]
    done = exchange(made[0], SHEETS)
    return tuple(deliver(done))


def solution(mesh):
    in_specs = (
        P("col", "row", None),
        P("row", "col", None, None, None),
        P("row", "col", None, None),
        P("row", "col"),
    )
    out_specs = (P("col", "row", None), P("col", "row", None))
    return jax.shard_map(
        shards, mesh=mesh, in_specs=in_specs, out_specs=out_specs, check_vma=False
    )
```

```python
import functools

import jax
import jax.numpy as jnp
from jax import lax
from jax.experimental import pallas as pl
from jax.experimental.pallas import tpu as pltpu
from jax.sharding import PartitionSpec as P

ITERS = 3
DIFFUSION = 0.8
RC = ("row", "col")


def split_id(device):
    r, c = divmod(device, 16)
    yh, x = divmod(r, 4)
    yl, q = divmod(c, 8)
    return yh * 2 + yl, x, q // 2, q % 2


def device_id(y, x, z, k):
    return ((y // 2) * 4 + x) * 16 + (y % 2) * 8 + z * 2 + k


def groups_by(key):
    groups = {}
    for device in range(128):
        groups.setdefault(key(*split_id(device)), []).append(device)
    return list(groups.values())


PLANES = groups_by(lambda y, x, z, k: (y, k))
SHEETS = groups_by(lambda y, x, z, k: (x, k))


def shift_y(d):
    pairs = []
    for device in range(128):
        y, x, z, k = split_id(device)
        pairs.append((device, device_id((y + d) % 4, x, z, k)))
    return pairs


SWAP = [(device, device ^ 1) for device in range(128)]


def exchange(send, groups):
    return lax.all_to_all(send, RC, 0, 0, axis_index_groups=groups, tiled=True)


def call(body, limit=16, **kw):
    return pl.pallas_call(
        body, compiler_params=pltpu.CompilerParams(vmem_limit_bytes=limit * 2**20), **kw
    )


EARLY = ((0, 0), (0, 1), (1, 0), (3, 1))
LATE = ((2, 0), (1, 1), (2, 1), (3, 0))


def corners(codes, back, half):
    y = (codes[64] - back) & 3
    row = (half ^ codes[65]) * 1024 + (y >> 1) * 256
    col = (y & 1) * 256
    for j in range(2):
        for i in range(2):
            at = pl.ds(pl.multiple_of(row + j * 512, 256), 256)
            by = pl.ds(pl.multiple_of(col + i * 512, 256), 256)
            yield j, i, at, by


def fill(codes, ref, first, back, half, hi, lo, work):
    work[...] = jnp.zeros_like(work)
    base = ((codes[64] - back) & 3) * 16 + half * 8
    for b in range(8):
        code = codes[base + b]

        @pl.when(code >= 0)
        def _(b=b, code=code):
            row, col = code >> 3, code & 7
            ro = pl.multiple_of((((row >> 2) & 1) * 2 + (row & 1)) * 128, 128)
            co = pl.multiple_of(((col >> 2) * 2 + (col & 1)) * 128, 128)
            work[pl.ds(ro, 128), pl.ds(co, 128)] += ref[first + b]

    for j, i, at, by in corners(codes, back, half):
        top, rest = parted(work[j * 256 : (j + 1) * 256, i * 256 : (i + 1) * 256])
        hi[at, by] = top
        lo[at, by] = rest


def early_body(codes, own0, own1, left0, right1, recv, hi, lo, share, work):
    share[...] = recv[:, :64, :]
    for ref, place in zip((own0, own1, left0, right1), EARLY):
        fill(codes, ref, 0, *place, hi, lo, work)


def late_body(codes, wave_in, back_in, hi0, lo0, hi, lo, work, wave, back, sems):
    copies = (
        pltpu.make_async_copy(wave_in, wave, sems.at[0]),
        pltpu.make_async_copy(back_in, back, sems.at[1]),
    )
    for copy in copies:
        copy.start()
    for place in EARLY:
        for _, _, at, by in corners(codes, *place):
            hi[at, by] = hi0[at, by]
            lo[at, by] = lo0[at, by]
    copies[0].wait()
    fill(codes, wave, 0, *LATE[0], hi, lo, work)
    fill(codes, wave, 8, *LATE[1], hi, lo, work)
    copies[1].wait()
    fill(codes, back, 0, *LATE[2], hi, lo, work)
    fill(codes, back, 8, *LATE[3], hi, lo, work)


VMEM = pl.BlockSpec(memory_space=pltpu.VMEM)
HBM = pl.BlockSpec(memory_space=pltpu.HBM)


SMEM = pl.BlockSpec(memory_space=pltpu.SMEM)
HALF = jax.ShapeDtypeStruct((2048, 1024), jnp.bfloat16)


def early(codes, *operands):
    return call(
        early_body,
        out_shape=(HALF, HALF, jax.ShapeDtypeStruct((16, 64, 128), jnp.float32)),
        in_specs=[SMEM] + [VMEM] * 5,
        out_specs=(VMEM,) * 3,
        scratch_shapes=[pltpu.VMEM((512, 512), jnp.float32)],
        name="early",
    )(codes, *operands)


def late(codes, *operands):
    return call(
        late_body,
        out_shape=(HALF, HALF),
        in_specs=[SMEM, HBM, HBM, VMEM, VMEM],
        out_specs=(VMEM,) * 2,
        scratch_shapes=[pltpu.VMEM((512, 512), jnp.float32)]
        + [pltpu.VMEM((16, 128, 128), jnp.float32)] * 2
        + [pltpu.SemaphoreType.DMA((2,))],
        name="late",
    )(codes, *operands)


def parted(value):
    top = value.astype(jnp.bfloat16)
    return top, (value - top.astype(jnp.float32)).astype(jnp.bfloat16)


def dot(a, b):
    return jnp.dot(a, b, preferred_element_type=jnp.float32)


def chunk(ref, j):
    return ref[:, j * 16 : j * 16 + 16, :].reshape(256, 128)


def part_right(recv, right):
    for s in range(4):
        top, rest = parted(chunk(recv, 4 + s))
        right[pl.ds(s * 256, 256), :128] = top
        right[pl.ds(s * 256, 256), 128:] = rest


def forward(hi, lo, right):
    wide = dot(hi, right[...])
    return wide[:, :128] + wide[:, 128:] + dot(lo, right[:, :128])


def mate_body(recv, hi, lo, out, right):
    part_right(recv, right)
    for i in range(2):
        rows = slice(1024 + i * 512, 1536 + i * 512)
        out[i * 512 : (i + 1) * 512, :] = forward(hi[rows, :], lo[rows, :], right)


def mate(recv, hi, lo):
    return call(
        mate_body,
        out_shape=jax.ShapeDtypeStruct((1024, 128), jnp.float32),
        in_specs=[VMEM] * 3,
        out_specs=VMEM,
        scratch_shapes=[pltpu.VMEM((1024, 256), jnp.bfloat16)],
        name="mate",
    )(recv, hi, lo)


def mirror_body(recv, other, hi, lo, sums, out, scalars, back):
    for i in range(4):
        ref = (recv, other)[i // 2]
        pairs = [parted(chunk(ref, (i % 2) * 2 + c).T) for c in range(2)]
        top = jnp.concatenate([pair[0] for pair in pairs], axis=1)
        rest = jnp.concatenate([pair[1] for pair in pairs], axis=1)
        rows = slice(i * 512, (i + 1) * 512)
        wide = dot(jnp.concatenate([top, rest], axis=0), hi[rows, :])
        part = wide[:128] + wide[128:] + dot(top, lo[rows, :])
        back[...] = part if i == 0 else back[...] + part
    out[...] = back[...].T
    curve = jnp.zeros((8, 128), jnp.float32)
    for s in range(4):
        piece = chunk(recv, 4 + s) * out[s * 256 : (s + 1) * 256]
        curve = curve + jnp.sum(piece.reshape(32, 8, 128), axis=0)
    place = lax.broadcasted_iota(jnp.int32, (8, 128), 0)
    scalars[...] = jnp.where(place == 2, row_sum(curve) * (2 * DIFFUSION), sums[...])


def mirror(recv, other, hi, lo, sums):
    return call(
        mirror_body,
        out_shape=(
            jax.ShapeDtypeStruct((1024, 128), jnp.float32),
            jax.ShapeDtypeStruct((8, 128), jnp.float32),
        ),
        in_specs=[VMEM] * 5,
        out_specs=(VMEM, VMEM),
        scratch_shapes=[pltpu.VMEM((128, 1024), jnp.float32)],
        name="mirror",
    )(recv, other, hi, lo, sums)


def own_body(recv, hi, lo, after, out, right):
    part_right(recv, right)
    for i in range(2):
        rows = slice(i * 512, (i + 1) * 512)
        out[rows, :] = forward(hi[rows, :], lo[rows, :], right)


def own_rows(recv, hi, lo, after):
    return call(
        own_body,
        out_shape=jax.ShapeDtypeStruct((1024, 128), jnp.float32),
        in_specs=[VMEM] * 4,
        out_specs=VMEM,
        scratch_shapes=[pltpu.VMEM((1024, 256), jnp.bfloat16)],
        name="own_rows",
    )(recv, hi, lo, after)


def join_body(ours, theirs, mirrored, mine, mates, out):
    for s in range(4):
        rows = slice(s * 256, (s + 1) * 256)
        part = ours[rows, :] + theirs[rows, :]
        out[:, s * 16 : s * 16 + 16, :] = part.reshape(16, 16, 128)
        out[:, 64 + s * 16 : 80 + s * 16, :] = mirrored[rows, :].reshape(16, 16, 128)
    row = mine[...] + mates[...]
    out[:, 128:136, :] = jnp.broadcast_to(row[None], (16, 8, 128))


def join(ours, theirs, mirrored, mine, mates):
    return call(
        join_body,
        out_shape=jax.ShapeDtypeStruct((16, 136, 128), jnp.float32),
        in_specs=[VMEM] * 5,
        out_specs=VMEM,
        name="join",
    )(ours, theirs, mirrored, mine, mates)


def multiply(recv, share, sums, hi, lo):
    other = lax.ppermute(share, RC, SWAP)
    theirs = lax.ppermute(mate(recv, hi, lo), RC, SWAP)
    mirrored, mine = mirror(recv, other, hi, lo, sums)
    mates = lax.ppermute(mine, RC, SWAP)
    ours = own_rows(recv, hi, lo, mine)
    return join(ours, theirs, mirrored, mine, mates)


def spread(field, send):
    for s in range(4):
        for g in range(4):
            piece = field(s, g)
            for other in range(4):
                send[g * 4 + other, s * 16 : s * 16 + 16, :] = piece
                send[other * 4 + g, 64 + s * 16 : 80 + s * 16, :] = piece


def row_sum(value):
    return jnp.sum(value, axis=0, keepdims=True)


def rows_of(*rows):
    place = lax.broadcasted_iota(jnp.int32, (8, 128), 0)
    out = jnp.zeros((8, 128), jnp.float32)
    for i, row in enumerate(rows):
        out = jnp.where(place == i, row, out)
    return out


def start_body(recv, left0, own1, right1, own0, send, sums, wave, back, work, sems):
    pieces = ((left0, wave, 0), (own1, wave, 8), (right1, back, 0), (own0, back, 8))
    copies = [
        pltpu.make_async_copy(src, dst.at[pl.ds(first, 8)], sems.at[i])
        for i, (src, dst, first) in enumerate(pieces)
    ]
    for copy in copies:
        copy.start()
    spread(lambda s, g: recv[s * 4 + g, :16], work)
    copies.append(pltpu.make_async_copy(work, send, sems.at[4]))
    copies[-1].start()
    square = jnp.zeros((16, 128), jnp.float32)
    for i in range(16):
        piece = recv[i, :16]
        square = square + piece * piece
    sums[...] = rows_of(row_sum(square))
    for copy in copies:
        copy.wait()


def start(*operands):
    big = jax.ShapeDtypeStruct((16, 128, 128), jnp.float32)
    small = jax.ShapeDtypeStruct((8, 128), jnp.float32)
    return call(
        start_body,
        out_shape=(big, small, big, big),
        in_specs=[VMEM] * 5,
        out_specs=(HBM, VMEM, HBM, HBM),
        scratch_shapes=[
            pltpu.VMEM((16, 128, 128), jnp.float32),
            pltpu.SemaphoreType.DMA((5,)),
        ],
        name="start",
    )(*operands)


def update_body(step, *refs):
    if step == 0:
        recv, residual = refs[:2]
        outs = refs[2:]
    else:
        recv, residual, direction, image, ranking, last = refs[:6]
        outs = refs[6:]
    total = jnp.zeros((8, 128), jnp.float32)
    for i in range(16):
        total = total + recv[i, 128:136]
    now = total[0:1]
    curve = now - total[2:3]
    if step > 0:
        beta = now / last[0:1]
        curve = curve + 2.0 * beta * total[1:2] + beta * beta * last[1:2]
    alpha = now / curve
    final = step + 1 == ITERS
    square = jnp.zeros((16, 128), jnp.float32)
    cross = jnp.zeros((16, 128), jnp.float32)
    for s in range(4):
        for g in range(4):
            acc = jnp.zeros((16, 128), jnp.float32)
            for other in range(4):
                acc = acc + recv[g * 4 + other, s * 16 : s * 16 + 16]
                acc = acc + recv[other * 4 + g, 64 + s * 16 : 80 + s * 16]
            i = s * 4 + g
            rest = residual[i, :16]
            aim = rest
            made = rest - DIFFUSION * acc
            if step > 0:
                aim = aim + beta * direction[i]
                made = made + beta * image[i]
            ranked = alpha * aim
            if step > 0:
                ranked = ranked + ranking[i]
            rest = rest - alpha * made
            if final:
                outs[0][i, 0] = ranked
                outs[0][i, 1] = rest
            else:
                send, new_residual, new_direction, new_image, new_ranking = outs[:5]
                new_residual[i] = rest
                new_direction[i] = aim
                new_image[i] = made
                new_ranking[i] = ranked
                square = square + rest * rest
                cross = cross + rest * made
    if not final:
        spread(lambda s, g: new_residual[s * 4 + g], send)
        outs[5][...] = rows_of(now, curve)
        outs[6][...] = rows_of(row_sum(square), row_sum(cross))


def update(step, *operands):
    field = jax.ShapeDtypeStruct((16, 16, 128), jnp.float32)
    small = jax.ShapeDtypeStruct((8, 128), jnp.float32)
    if step + 1 == ITERS:
        shapes = [jax.ShapeDtypeStruct((16, 2, 16, 128), jnp.float32)]
    else:
        send = jax.ShapeDtypeStruct((16, 128, 128), jnp.float32)
        shapes = [send, field, field, field, field, small, small]
    return call(
        functools.partial(update_body, step), out_shape=shapes, name="update"
    )(*operands)


def deliver_body(recv, *outs):
    for y in range(4):
        for z in range(4):
            for which, out in enumerate(outs):
                out[0, z * 16 : z * 16 + 16, y * 128 : y * 128 + 128] = recv[y * 4 + z, which]


def deliver(recv):
    out = jax.ShapeDtypeStruct((1, 64, 512), jnp.float32)
    return call(deliver_body, out_shape=(out, out), name="deliver")(recv)


def shards(right_side, affinity_blocks, block_coords, block_counts):
    r = lax.axis_index("row")
    c = lax.axis_index("col")
    yh, yl, z, k = r // 4, c // 8, (c // 2) % 4, c % 2
    own0 = affinity_blocks[0, 0]
    own1 = affinity_blocks[1, 0]
    left0 = lax.ppermute(own0, RC, shift_y(1))
    right1 = lax.ppermute(own1, RC, shift_y(3))

    br = block_coords[:, 0, :, 0]
    bc = block_coords[:, 0, :, 1]
    par = jnp.arange(2, dtype=jnp.int32)[:, None] ^ k
    row128 = par * 8 + ((br // 2) * 2 + yh) * 2 + br % 2
    col128 = ((bc // 2) * 2 + yl) * 2 + bc % 2
    live = jnp.arange(8, dtype=jnp.int32)[None, :] < block_counts
    code = jnp.where(live, row128 * 8 + col128, -1).astype(jnp.float32)
    meta = jnp.pad(code.reshape(1, 16), ((0, 7), (0, 112)))

    send = right_side.reshape(4, 16, 4, 128).transpose(2, 0, 1, 3).reshape(16, 16, 128)
    send = jnp.concatenate([send, jnp.broadcast_to(meta[None], (16, 8, 128))], axis=1)
    recv = exchange(send, SHEETS)
    codes = lax.dynamic_slice(recv.reshape(4, 4, 24, 128), (0, z, 16, 0), (4, 1, 1, 16))
    codes = jnp.concatenate(
        [codes.reshape(64).astype(jnp.int32), jnp.stack([yh * 2 + yl, k]).astype(jnp.int32)]
    )

    send, sums, wave, back = start(recv, left0, own1, right1, own0)
    state = (recv,)
    wave = lax.ppermute(wave, RC, shift_y(1))
    back = lax.ppermute(back, RC, shift_y(3))
    got = exchange(send, PLANES)
    hi, lo, share = early(codes, own0, own1, left0, right1, got)
    hi, lo = late(codes, wave, back, hi, lo)
    for step in range(ITERS):
        if step:
            got = share = exchange(send, PLANES)
        products = exchange(multiply(got, share, sums, hi, lo), PLANES)
        made = update(step, products, *state)
        if step + 1 < ITERS:
            send, sums = made[0], made[6]
            state = made[1:6]
    done = exchange(made[0], SHEETS)
    return tuple(deliver(done))


def solution(mesh):
    in_specs = (
        P("col", "row", None),
        P("row", "col", None, None, None),
        P("row", "col", None, None),
        P("row", "col"),
    )
    out_specs = (P("col", "row", None), P("col", "row", None))
    return jax.shard_map(
        shards, mesh=mesh, in_specs=in_specs, out_specs=out_specs, check_vma=False
    )
```

```python
import functools

import jax
import jax.numpy as jnp
from jax import lax
from jax.experimental import pallas as pl
from jax.experimental.pallas import tpu as pltpu
from jax.sharding import PartitionSpec as P

ITERS = 3
DIFFUSION = 0.8
RC = ("row", "col")


def split_id(device):
    r, c = divmod(device, 16)
    yh, x = divmod(r, 4)
    yl, q = divmod(c, 8)
    return yh * 2 + yl, x, q // 2, q % 2


def device_id(y, x, z, k):
    return ((y // 2) * 4 + x) * 16 + (y % 2) * 8 + z * 2 + k


def groups_by(key):
    groups = {}
    for device in range(128):
        groups.setdefault(key(*split_id(device)), []).append(device)
    return list(groups.values())


PLANES = groups_by(lambda y, x, z, k: (y, k))
SHEETS = groups_by(lambda y, x, z, k: (x, k))


def shift_y(d):
    pairs = []
    for device in range(128):
        y, x, z, k = split_id(device)
        pairs.append((device, device_id((y + d) % 4, x, z, k)))
    return pairs


SWAP = [(device, device ^ 1) for device in range(128)]


def exchange(send, groups):
    return lax.all_to_all(send, RC, 0, 0, axis_index_groups=groups, tiled=True)


def call(body, limit=16, **kw):
    return pl.pallas_call(
        body, compiler_params=pltpu.CompilerParams(vmem_limit_bytes=limit * 2**20), **kw
    )


EARLY = ((0, 0), (0, 1), (1, 0), (3, 1))
LATE = ((2, 0), (1, 1), (2, 1), (3, 0))


def corners(codes, back, half):
    y = (codes[64] - back) & 3
    row = (half ^ codes[65]) * 1024 + (y >> 1) * 256
    col = (y & 1) * 256
    for j in range(2):
        for i in range(2):
            at = pl.ds(pl.multiple_of(row + j * 512, 256), 256)
            by = pl.ds(pl.multiple_of(col + i * 512, 256), 256)
            yield j, i, at, by


def fill(codes, ref, first, back, half, hi, lo, work):
    work[...] = jnp.zeros_like(work)
    base = ((codes[64] - back) & 3) * 16 + half * 8
    for b in range(8):
        code = codes[base + b]

        @pl.when(code >= 0)
        def _(b=b, code=code):
            row, col = code >> 3, code & 7
            ro = pl.multiple_of((((row >> 2) & 1) * 2 + (row & 1)) * 128, 128)
            co = pl.multiple_of(((col >> 2) * 2 + (col & 1)) * 128, 128)
            work[pl.ds(ro, 128), pl.ds(co, 128)] += ref[first + b]

    for j, i, at, by in corners(codes, back, half):
        top, rest = parted(work[j * 256 : (j + 1) * 256, i * 256 : (i + 1) * 256])
        hi[at, by] = top
        lo[at, by] = rest


def early_body(codes, own0, own1, left0, right1, recv, hi, lo, share, work):
    share[...] = recv[:, :64, :]
    for ref, place in zip((own0, own1, left0, right1), EARLY):
        fill(codes, ref, 0, *place, hi, lo, work)


def late_body(codes, wave_in, back_in, hi0, lo0, hi, lo, work, wave, back, sems):
    copies = (
        pltpu.make_async_copy(wave_in, wave, sems.at[0]),
        pltpu.make_async_copy(back_in, back, sems.at[1]),
    )
    for copy in copies:
        copy.start()
    for place in EARLY:
        for _, _, at, by in corners(codes, *place):
            hi[at, by] = hi0[at, by]
            lo[at, by] = lo0[at, by]
    copies[0].wait()
    fill(codes, wave, 0, *LATE[0], hi, lo, work)
    fill(codes, wave, 8, *LATE[1], hi, lo, work)
    copies[1].wait()
    fill(codes, back, 0, *LATE[2], hi, lo, work)
    fill(codes, back, 8, *LATE[3], hi, lo, work)


VMEM = pl.BlockSpec(memory_space=pltpu.VMEM)
HBM = pl.BlockSpec(memory_space=pltpu.HBM)


SMEM = pl.BlockSpec(memory_space=pltpu.SMEM)
HALF = jax.ShapeDtypeStruct((2048, 1024), jnp.bfloat16)


def early(codes, *operands):
    return call(
        early_body,
        out_shape=(HALF, HALF, jax.ShapeDtypeStruct((16, 64, 128), jnp.float32)),
        in_specs=[SMEM] + [VMEM] * 5,
        out_specs=(VMEM,) * 3,
        scratch_shapes=[pltpu.VMEM((512, 512), jnp.float32)],
        name="early",
    )(codes, *operands)


def late(codes, *operands):
    return call(
        late_body,
        out_shape=(HALF, HALF),
        in_specs=[SMEM, HBM, HBM, VMEM, VMEM],
        out_specs=(VMEM,) * 2,
        scratch_shapes=[pltpu.VMEM((512, 512), jnp.float32)]
        + [pltpu.VMEM((16, 128, 128), jnp.float32)] * 2
        + [pltpu.SemaphoreType.DMA((2,))],
        name="late",
    )(codes, *operands)


def parted(value):
    top = value.astype(jnp.bfloat16)
    return top, (value - top.astype(jnp.float32)).astype(jnp.bfloat16)


def dot(a, b):
    return jnp.dot(a, b, preferred_element_type=jnp.float32)


def chunk(ref, j):
    return ref[:, j * 16 : j * 16 + 16, :].reshape(256, 128)


def part_right(recv, right):
    for s in range(4):
        top, rest = parted(chunk(recv, 4 + s))
        right[pl.ds(s * 256, 256), :128] = top
        right[pl.ds(s * 256, 256), 128:] = rest


def forward(hi, lo, right):
    wide = dot(hi, right[...])
    return wide[:, :128] + wide[:, 128:] + dot(lo, right[:, :128])


def mate_body(recv, hi, lo, out, right):
    part_right(recv, right)
    for i in range(2):
        rows = slice(1024 + i * 512, 1536 + i * 512)
        out[i * 512 : (i + 1) * 512, :] = forward(hi[rows, :], lo[rows, :], right)


def mate(recv, hi, lo):
    return call(
        mate_body,
        out_shape=jax.ShapeDtypeStruct((1024, 128), jnp.float32),
        in_specs=[VMEM] * 3,
        out_specs=VMEM,
        scratch_shapes=[pltpu.VMEM((1024, 256), jnp.bfloat16)],
        name="mate",
    )(recv, hi, lo)


def mirror_body(recv, other, hi, lo, sums, out, scalars, back):
    for i in range(4):
        ref = (recv, other)[i // 2]
        pairs = [parted(chunk(ref, (i % 2) * 2 + c).T) for c in range(2)]
        top = jnp.concatenate([pair[0] for pair in pairs], axis=1)
        rest = jnp.concatenate([pair[1] for pair in pairs], axis=1)
        rows = slice(i * 512, (i + 1) * 512)
        wide = dot(jnp.concatenate([top, rest], axis=0), hi[rows, :])
        part = wide[:128] + wide[128:] + dot(top, lo[rows, :])
        back[...] = part if i == 0 else back[...] + part
    out[...] = back[...].T
    curve = jnp.zeros((8, 128), jnp.float32)
    for s in range(4):
        piece = chunk(recv, 4 + s) * out[s * 256 : (s + 1) * 256]
        curve = curve + jnp.sum(piece.reshape(32, 8, 128), axis=0)
    place = lax.broadcasted_iota(jnp.int32, (8, 128), 0)
    scalars[...] = jnp.where(place == 2, row_sum(curve) * (2 * DIFFUSION), sums[...])


def mirror(recv, other, hi, lo, sums):
    return call(
        mirror_body,
        out_shape=(
            jax.ShapeDtypeStruct((1024, 128), jnp.float32),
            jax.ShapeDtypeStruct((8, 128), jnp.float32),
        ),
        in_specs=[VMEM] * 5,
        out_specs=(VMEM, VMEM),
        scratch_shapes=[pltpu.VMEM((128, 1024), jnp.float32)],
        name="mirror",
    )(recv, other, hi, lo, sums)


def own_body(recv, hi, lo, after, out, right):
    part_right(recv, right)
    for i in range(2):
        rows = slice(i * 512, (i + 1) * 512)
        out[rows, :] = forward(hi[rows, :], lo[rows, :], right)


def own_rows(recv, hi, lo, after):
    return call(
        own_body,
        out_shape=jax.ShapeDtypeStruct((1024, 128), jnp.float32),
        in_specs=[VMEM] * 4,
        out_specs=VMEM,
        scratch_shapes=[pltpu.VMEM((1024, 256), jnp.bfloat16)],
        name="own_rows",
    )(recv, hi, lo, after)


def join_body(ours, theirs, mirrored, mine, mates, out):
    for s in range(4):
        rows = slice(s * 256, (s + 1) * 256)
        part = ours[rows, :] + theirs[rows, :]
        out[:, s * 16 : s * 16 + 16, :] = part.reshape(16, 16, 128)
        out[:, 64 + s * 16 : 80 + s * 16, :] = mirrored[rows, :].reshape(16, 16, 128)
    row = mine[...] + mates[...]
    out[:, 128:136, :] = jnp.broadcast_to(row[None], (16, 8, 128))


def join(ours, theirs, mirrored, mine, mates):
    return call(
        join_body,
        out_shape=jax.ShapeDtypeStruct((16, 136, 128), jnp.float32),
        in_specs=[VMEM] * 5,
        out_specs=VMEM,
        name="join",
    )(ours, theirs, mirrored, mine, mates)


def multiply(recv, share, sums, hi, lo):
    other = lax.ppermute(share, RC, SWAP)
    theirs = lax.ppermute(mate(recv, hi, lo), RC, SWAP)
    mirrored, mine = mirror(recv, other, hi, lo, sums)
    mates = lax.ppermute(mine, RC, SWAP)
    ours = own_rows(recv, hi, lo, mine)
    return join(ours, theirs, mirrored, mine, mates)


def spread(field, send):
    for s in range(4):
        for g in range(4):
            piece = field(s, g)
            for other in range(4):
                send[g * 4 + other, s * 16 : s * 16 + 16, :] = piece
                send[other * 4 + g, 64 + s * 16 : 80 + s * 16, :] = piece


def row_sum(value):
    return jnp.sum(value, axis=0, keepdims=True)


def rows_of(*rows):
    place = lax.broadcasted_iota(jnp.int32, (8, 128), 0)
    out = jnp.zeros((8, 128), jnp.float32)
    for i, row in enumerate(rows):
        out = jnp.where(place == i, row, out)
    return out


def pack_body(left0, own1, right1, own0, recv, wave, back, sems):
    pieces = ((left0, wave, 0), (own1, wave, 8), (right1, back, 0), (own0, back, 8))
    copies = [
        pltpu.make_async_copy(src, dst.at[pl.ds(first, 8)], sems.at[i])
        for i, (src, dst, first) in enumerate(pieces)
    ]
    for copy in copies:
        copy.start()
    for copy in copies:
        copy.wait()


def pack(*operands):
    big = jax.ShapeDtypeStruct((16, 128, 128), jnp.float32)
    return call(
        pack_body,
        out_shape=(big, big),
        in_specs=[VMEM] * 5,
        out_specs=(HBM, HBM),
        scratch_shapes=[pltpu.SemaphoreType.DMA((4,))],
        name="pack",
    )(*operands)


def start_body(recv, send, sums):
    spread(lambda s, g: recv[s * 4 + g, :16], send)
    square = jnp.zeros((16, 128), jnp.float32)
    for i in range(16):
        piece = recv[i, :16]
        square = square + piece * piece
    sums[...] = rows_of(row_sum(square))


def start(recv):
    big = jax.ShapeDtypeStruct((16, 128, 128), jnp.float32)
    small = jax.ShapeDtypeStruct((8, 128), jnp.float32)
    return call(
        start_body,
        out_shape=(big, small),
        in_specs=[VMEM],
        out_specs=(VMEM, VMEM),
        name="start",
    )(recv)


def update_body(step, *refs):
    if step == 0:
        recv, residual = refs[:2]
        outs = refs[2:]
    else:
        recv, residual, direction, image, ranking, last = refs[:6]
        outs = refs[6:]
    total = jnp.zeros((8, 128), jnp.float32)
    for i in range(16):
        total = total + recv[i, 128:136]
    now = total[0:1]
    curve = now - total[2:3]
    if step > 0:
        beta = now / last[0:1]
        curve = curve + 2.0 * beta * total[1:2] + beta * beta * last[1:2]
    alpha = now / curve
    final = step + 1 == ITERS
    square = jnp.zeros((16, 128), jnp.float32)
    cross = jnp.zeros((16, 128), jnp.float32)
    for s in range(4):
        for g in range(4):
            acc = jnp.zeros((16, 128), jnp.float32)
            for other in range(4):
                acc = acc + recv[g * 4 + other, s * 16 : s * 16 + 16]
                acc = acc + recv[other * 4 + g, 64 + s * 16 : 80 + s * 16]
            i = s * 4 + g
            rest = residual[i, :16]
            aim = rest
            made = rest - DIFFUSION * acc
            if step > 0:
                aim = aim + beta * direction[i]
                made = made + beta * image[i]
            ranked = alpha * aim
            if step > 0:
                ranked = ranked + ranking[i]
            rest = rest - alpha * made
            if final:
                outs[0][i, 0] = ranked
                outs[0][i, 1] = rest
            else:
                send, new_residual, new_direction, new_image, new_ranking = outs[:5]
                new_residual[i] = rest
                new_direction[i] = aim
                new_image[i] = made
                new_ranking[i] = ranked
                square = square + rest * rest
                cross = cross + rest * made
    if not final:
        spread(lambda s, g: new_residual[s * 4 + g], send)
        outs[5][...] = rows_of(now, curve)
        outs[6][...] = rows_of(row_sum(square), row_sum(cross))


def update(step, *operands):
    field = jax.ShapeDtypeStruct((16, 16, 128), jnp.float32)
    small = jax.ShapeDtypeStruct((8, 128), jnp.float32)
    if step + 1 == ITERS:
        shapes = [jax.ShapeDtypeStruct((16, 2, 16, 128), jnp.float32)]
    else:
        send = jax.ShapeDtypeStruct((16, 128, 128), jnp.float32)
        shapes = [send, field, field, field, field, small, small]
    return call(
        functools.partial(update_body, step), out_shape=shapes, name="update"
    )(*operands)


def deliver_body(recv, *outs):
    for y in range(4):
        for z in range(4):
            for which, out in enumerate(outs):
                out[0, z * 16 : z * 16 + 16, y * 128 : y * 128 + 128] = recv[y * 4 + z, which]


def deliver(recv):
    out = jax.ShapeDtypeStruct((1, 64, 512), jnp.float32)
    return call(deliver_body, out_shape=(out, out), name="deliver")(recv)


def shards(right_side, affinity_blocks, block_coords, block_counts):
    r = lax.axis_index("row")
    c = lax.axis_index("col")
    yh, yl, z, k = r // 4, c // 8, (c // 2) % 4, c % 2
    own0 = affinity_blocks[0, 0]
    own1 = affinity_blocks[1, 0]
    left0 = lax.ppermute(own0, RC, shift_y(1))
    right1 = lax.ppermute(own1, RC, shift_y(3))

    br = block_coords[:, 0, :, 0]
    bc = block_coords[:, 0, :, 1]
    par = jnp.arange(2, dtype=jnp.int32)[:, None] ^ k
    row128 = par * 8 + ((br // 2) * 2 + yh) * 2 + br % 2
    col128 = ((bc // 2) * 2 + yl) * 2 + bc % 2
    live = jnp.arange(8, dtype=jnp.int32)[None, :] < block_counts
    code = jnp.where(live, row128 * 8 + col128, -1).astype(jnp.float32)
    meta = jnp.pad(code.reshape(1, 16), ((0, 7), (0, 112)))

    send = right_side.reshape(4, 16, 4, 128).transpose(2, 0, 1, 3).reshape(16, 16, 128)
    send = jnp.concatenate([send, jnp.broadcast_to(meta[None], (16, 8, 128))], axis=1)
    recv = exchange(send, SHEETS)
    codes = lax.dynamic_slice(recv.reshape(4, 4, 24, 128), (0, z, 16, 0), (4, 1, 1, 16))
    codes = jnp.concatenate(
        [codes.reshape(64).astype(jnp.int32), jnp.stack([yh * 2 + yl, k]).astype(jnp.int32)]
    )

    wave, back = pack(left0, own1, right1, own0, recv)
    send, sums = start(recv)
    state = (recv,)
    wave = lax.ppermute(wave, RC, shift_y(1))
    back = lax.ppermute(back, RC, shift_y(3))
    got = exchange(send, PLANES)
    hi, lo, share = early(codes, own0, own1, left0, right1, got)
    hi, lo = late(codes, wave, back, hi, lo)
    for step in range(ITERS):
        if step:
            got = share = exchange(send, PLANES)
        products = exchange(multiply(got, share, sums, hi, lo), PLANES)
        made = update(step, products, *state)
        if step + 1 < ITERS:
            send, sums = made[0], made[6]
            state = made[1:6]
    done = exchange(made[0], SHEETS)
    return tuple(deliver(done))


def solution(mesh):
    in_specs = (
        P("col", "row", None),
        P("row", "col", None, None, None),
        P("row", "col", None, None),
        P("row", "col"),
    )
    out_specs = (P("col", "row", None), P("col", "row", None))
    return jax.shard_map(
        shards, mesh=mesh, in_specs=in_specs, out_specs=out_specs, check_vma=False
    )
```

```python
import functools

import jax
import jax.numpy as jnp
from jax import lax
from jax.experimental import pallas as pl
from jax.experimental.pallas import tpu as pltpu
from jax.sharding import PartitionSpec as P

ITERS = 3
DIFFUSION = 0.8
RC = ("row", "col")


def split_id(device):
    r, c = divmod(device, 16)
    yh, x = divmod(r, 4)
    yl, q = divmod(c, 8)
    return yh * 2 + yl, x, q // 2, q % 2


def device_id(y, x, z, k):
    return ((y // 2) * 4 + x) * 16 + (y % 2) * 8 + z * 2 + k


def groups_by(key):
    groups = {}
    for device in range(128):
        groups.setdefault(key(*split_id(device)), []).append(device)
    return list(groups.values())


PLANES = groups_by(lambda y, x, z, k: (y, k))
SHEETS = groups_by(lambda y, x, z, k: (x, k))


def shift_y(d):
    pairs = []
    for device in range(128):
        y, x, z, k = split_id(device)
        pairs.append((device, device_id((y + d) % 4, x, z, k)))
    return pairs


SWAP = [(device, device ^ 1) for device in range(128)]


def exchange(send, groups):
    return lax.all_to_all(send, RC, 0, 0, axis_index_groups=groups, tiled=True)


def call(body, limit=16, **kw):
    return pl.pallas_call(
        body, compiler_params=pltpu.CompilerParams(vmem_limit_bytes=limit * 2**20), **kw
    )


EARLY = ((0, 0), (0, 1), (1, 0), (3, 1))
LATE = ((2, 0), (1, 1), (2, 1), (3, 0))


def corners(codes, back, half):
    y = (codes[64] - back) & 3
    row = (half ^ codes[65]) * 1024 + (y >> 1) * 256
    col = (y & 1) * 256
    for j in range(2):
        for i in range(2):
            at = pl.ds(pl.multiple_of(row + j * 512, 256), 256)
            by = pl.ds(pl.multiple_of(col + i * 512, 256), 256)
            yield j, i, at, by


def fill(codes, ref, first, back, half, hi, lo, work):
    work[...] = jnp.zeros_like(work)
    base = ((codes[64] - back) & 3) * 16 + half * 8
    for b in range(8):
        code = codes[base + b]

        @pl.when(code >= 0)
        def _(b=b, code=code):
            row, col = code >> 3, code & 7
            ro = pl.multiple_of((((row >> 2) & 1) * 2 + (row & 1)) * 128, 128)
            co = pl.multiple_of(((col >> 2) * 2 + (col & 1)) * 128, 128)
            work[pl.ds(ro, 128), pl.ds(co, 128)] += ref[first + b]

    for j, i, at, by in corners(codes, back, half):
        top, rest = parted(work[j * 256 : (j + 1) * 256, i * 256 : (i + 1) * 256])
        hi[at, by] = top
        lo[at, by] = rest


def early_body(codes, own0, own1, left0, right1, recv, hi, lo, share, work):
    share[...] = recv[:, :64, :]
    for ref, place in zip((own0, own1, left0, right1), EARLY):
        fill(codes, ref, 0, *place, hi, lo, work)


def late_body(codes, wave_in, back_in, hi0, lo0, hi, lo, work, wave, back, sems):
    copies = (
        pltpu.make_async_copy(wave_in, wave, sems.at[0]),
        pltpu.make_async_copy(back_in, back, sems.at[1]),
    )
    for copy in copies:
        copy.start()
    for place in EARLY:
        for _, _, at, by in corners(codes, *place):
            hi[at, by] = hi0[at, by]
            lo[at, by] = lo0[at, by]
    copies[0].wait()
    fill(codes, wave, 0, *LATE[0], hi, lo, work)
    fill(codes, wave, 8, *LATE[1], hi, lo, work)
    copies[1].wait()
    fill(codes, back, 0, *LATE[2], hi, lo, work)
    fill(codes, back, 8, *LATE[3], hi, lo, work)


VMEM = pl.BlockSpec(memory_space=pltpu.VMEM)
HBM = pl.BlockSpec(memory_space=pltpu.HBM)


SMEM = pl.BlockSpec(memory_space=pltpu.SMEM)
HALF = jax.ShapeDtypeStruct((2048, 1024), jnp.bfloat16)


def early(codes, *operands):
    return call(
        early_body,
        out_shape=(HALF, HALF, jax.ShapeDtypeStruct((16, 64, 128), jnp.float32)),
        in_specs=[SMEM] + [VMEM] * 5,
        out_specs=(VMEM,) * 3,
        scratch_shapes=[pltpu.VMEM((512, 512), jnp.float32)],
        name="early",
    )(codes, *operands)


def late(codes, *operands):
    return call(
        late_body,
        out_shape=(HALF, HALF),
        in_specs=[SMEM, HBM, HBM, VMEM, VMEM],
        out_specs=(VMEM,) * 2,
        scratch_shapes=[pltpu.VMEM((512, 512), jnp.float32)]
        + [pltpu.VMEM((16, 128, 128), jnp.float32)] * 2
        + [pltpu.SemaphoreType.DMA((2,))],
        name="late",
    )(codes, *operands)


def parted(value):
    top = value.astype(jnp.bfloat16)
    return top, (value - top.astype(jnp.float32)).astype(jnp.bfloat16)


def dot(a, b):
    return jnp.dot(a, b, preferred_element_type=jnp.float32)


def chunk(ref, j):
    return ref[:, j * 16 : j * 16 + 16, :].reshape(256, 128)


def part_right(recv, right):
    for s in range(4):
        top, rest = parted(chunk(recv, 4 + s))
        right[pl.ds(s * 256, 256), :128] = top
        right[pl.ds(s * 256, 256), 128:] = rest


def forward(hi, lo, right):
    wide = dot(hi, right[...])
    return wide[:, :128] + wide[:, 128:] + dot(lo, right[:, :128])


def mate_body(recv, hi, lo, out, right):
    part_right(recv, right)
    for i in range(2):
        rows = slice(1024 + i * 512, 1536 + i * 512)
        out[i * 512 : (i + 1) * 512, :] = forward(hi[rows, :], lo[rows, :], right)


def mate(recv, hi, lo):
    return call(
        mate_body,
        out_shape=jax.ShapeDtypeStruct((1024, 128), jnp.float32),
        in_specs=[VMEM] * 3,
        out_specs=VMEM,
        scratch_shapes=[pltpu.VMEM((1024, 256), jnp.bfloat16)],
        name="mate",
    )(recv, hi, lo)


def mirror_body(recv, other, hi, lo, sums, after, out, scalars, back):
    for i in range(4):
        ref = (recv, other)[i // 2]
        pairs = [parted(chunk(ref, (i % 2) * 2 + c).T) for c in range(2)]
        top = jnp.concatenate([pair[0] for pair in pairs], axis=1)
        rest = jnp.concatenate([pair[1] for pair in pairs], axis=1)
        rows = slice(i * 512, (i + 1) * 512)
        wide = dot(jnp.concatenate([top, rest], axis=0), hi[rows, :])
        part = wide[:128] + wide[128:] + dot(top, lo[rows, :])
        back[...] = part if i == 0 else back[...] + part
    out[...] = back[...].T
    curve = jnp.zeros((8, 128), jnp.float32)
    for s in range(4):
        piece = chunk(recv, 4 + s) * out[s * 256 : (s + 1) * 256]
        curve = curve + jnp.sum(piece.reshape(32, 8, 128), axis=0)
    place = lax.broadcasted_iota(jnp.int32, (8, 128), 0)
    scalars[...] = jnp.where(place == 2, row_sum(curve) * (2 * DIFFUSION), sums[...])


def mirror(recv, other, hi, lo, sums, after):
    return call(
        mirror_body,
        out_shape=(
            jax.ShapeDtypeStruct((1024, 128), jnp.float32),
            jax.ShapeDtypeStruct((8, 128), jnp.float32),
        ),
        in_specs=[VMEM] * 6,
        out_specs=(VMEM, VMEM),
        scratch_shapes=[pltpu.VMEM((128, 1024), jnp.float32)],
        name="mirror",
    )(recv, other, hi, lo, sums, after)


def own_body(first, recv, hi, lo, after, out, right):
    part_right(recv, right)
    rows = slice(first, first + 512)
    out[...] = forward(hi[rows, :], lo[rows, :], right)


def own_rows(first, recv, hi, lo, after):
    return call(
        functools.partial(own_body, first),
        out_shape=jax.ShapeDtypeStruct((512, 128), jnp.float32),
        in_specs=[VMEM] * 4,
        out_specs=VMEM,
        scratch_shapes=[pltpu.VMEM((1024, 256), jnp.bfloat16)],
        name="own_rows",
    )(recv, hi, lo, after)


def join_body(ours0, ours1, theirs, mirrored, mine, mates, out):
    for s in range(4):
        rows = slice(s * 256, (s + 1) * 256)
        ours = (ours0, ours1)[s // 2]
        part = ours[(s % 2) * 256 : (s % 2) * 256 + 256, :] + theirs[rows, :]
        out[:, s * 16 : s * 16 + 16, :] = part.reshape(16, 16, 128)
        out[:, 64 + s * 16 : 80 + s * 16, :] = mirrored[rows, :].reshape(16, 16, 128)
    row = mine[...] + mates[...]
    out[:, 128:136, :] = jnp.broadcast_to(row[None], (16, 8, 128))


def join(ours0, ours1, theirs, mirrored, mine, mates):
    return call(
        join_body,
        out_shape=jax.ShapeDtypeStruct((16, 136, 128), jnp.float32),
        in_specs=[VMEM] * 6,
        out_specs=VMEM,
        name="join",
    )(ours0, ours1, theirs, mirrored, mine, mates)


def multiply(recv, share, sums, hi, lo):
    other = lax.ppermute(share, RC, SWAP)
    part = mate(recv, hi, lo)
    theirs = lax.ppermute(part, RC, SWAP)
    ours0 = own_rows(0, recv, hi, lo, part)
    mirrored, mine = mirror(recv, other, hi, lo, sums, ours0)
    mates = lax.ppermute(mine, RC, SWAP)
    ours1 = own_rows(512, recv, hi, lo, mine)
    return join(ours0, ours1, theirs, mirrored, mine, mates)


def spread(field, send):
    for s in range(4):
        for g in range(4):
            piece = field(s, g)
            for other in range(4):
                send[g * 4 + other, s * 16 : s * 16 + 16, :] = piece
                send[other * 4 + g, 64 + s * 16 : 80 + s * 16, :] = piece


def row_sum(value):
    return jnp.sum(value, axis=0, keepdims=True)


def rows_of(*rows):
    place = lax.broadcasted_iota(jnp.int32, (8, 128), 0)
    out = jnp.zeros((8, 128), jnp.float32)
    for i, row in enumerate(rows):
        out = jnp.where(place == i, row, out)
    return out


def halves_body(blocks, own0, own1, sems):
    copies = [
        pltpu.make_async_copy(blocks.at[i, 0], out, sems.at[i])
        for i, out in enumerate((own0, own1))
    ]
    for copy in copies:
        copy.start()
    for copy in copies:
        copy.wait()


def halves(blocks):
    half = jax.ShapeDtypeStruct((8, 128, 128), jnp.float32)
    return call(
        halves_body,
        out_shape=(half, half),
        in_specs=[HBM],
        out_specs=(VMEM, VMEM),
        scratch_shapes=[pltpu.SemaphoreType.DMA((2,))],
        name="halves",
    )(blocks)


def pack_body(left0, own1, right1, own0, recv, wave, back, sems):
    pieces = ((left0, wave, 0), (own1, wave, 8), (right1, back, 0), (own0, back, 8))
    copies = [
        pltpu.make_async_copy(src, dst.at[pl.ds(first, 8)], sems.at[i])
        for i, (src, dst, first) in enumerate(pieces)
    ]
    for copy in copies:
        copy.start()
    for copy in copies:
        copy.wait()


def pack(*operands):
    big = jax.ShapeDtypeStruct((16, 128, 128), jnp.float32)
    return call(
        pack_body,
        out_shape=(big, big),
        in_specs=[VMEM] * 5,
        out_specs=(HBM, HBM),
        scratch_shapes=[pltpu.SemaphoreType.DMA((4,))],
        name="pack",
    )(*operands)


def start_body(recv, send, sums):
    spread(lambda s, g: recv[s * 4 + g, :16], send)
    square = jnp.zeros((16, 128), jnp.float32)
    for i in range(16):
        piece = recv[i, :16]
        square = square + piece * piece
    sums[...] = rows_of(row_sum(square))


def start(recv):
    big = jax.ShapeDtypeStruct((16, 128, 128), jnp.float32)
    small = jax.ShapeDtypeStruct((8, 128), jnp.float32)
    return call(
        start_body,
        out_shape=(big, small),
        in_specs=[VMEM],
        out_specs=(VMEM, VMEM),
        name="start",
    )(recv)


def update_body(step, *refs):
    if step == 0:
        recv, residual = refs[:2]
        outs = refs[2:]
    else:
        recv, residual, direction, image, ranking, last = refs[:6]
        outs = refs[6:]
    total = jnp.zeros((8, 128), jnp.float32)
    for i in range(16):
        total = total + recv[i, 128:136]
    now = total[0:1]
    curve = now - total[2:3]
    if step > 0:
        beta = now / last[0:1]
        curve = curve + 2.0 * beta * total[1:2] + beta * beta * last[1:2]
    alpha = now / curve
    final = step + 1 == ITERS
    square = jnp.zeros((16, 128), jnp.float32)
    cross = jnp.zeros((16, 128), jnp.float32)
    for s in range(4):
        for g in range(4):
            acc = jnp.zeros((16, 128), jnp.float32)
            for other in range(4):
                acc = acc + recv[g * 4 + other, s * 16 : s * 16 + 16]
                acc = acc + recv[other * 4 + g, 64 + s * 16 : 80 + s * 16]
            i = s * 4 + g
            rest = residual[i, :16]
            aim = rest
            made = rest - DIFFUSION * acc
            if step > 0:
                aim = aim + beta * direction[i]
                made = made + beta * image[i]
            ranked = alpha * aim
            if step > 0:
                ranked = ranked + ranking[i]
            rest = rest - alpha * made
            if final:
                outs[0][i, 0] = ranked
                outs[0][i, 1] = rest
            else:
                send, new_residual, new_direction, new_image, new_ranking = outs[:5]
                new_residual[i] = rest
                new_direction[i] = aim
                new_image[i] = made
                new_ranking[i] = ranked
                square = square + rest * rest
                cross = cross + rest * made
    if not final:
        spread(lambda s, g: new_residual[s * 4 + g], send)
        outs[5][...] = rows_of(now, curve)
        outs[6][...] = rows_of(row_sum(square), row_sum(cross))


def update(step, *operands):
    field = jax.ShapeDtypeStruct((16, 16, 128), jnp.float32)
    small = jax.ShapeDtypeStruct((8, 128), jnp.float32)
    if step + 1 == ITERS:
        shapes = [jax.ShapeDtypeStruct((16, 2, 16, 128), jnp.float32)]
    else:
        send = jax.ShapeDtypeStruct((16, 128, 128), jnp.float32)
        shapes = [send, field, field, field, field, small, small]
    return call(
        functools.partial(update_body, step), out_shape=shapes, name="update"
    )(*operands)


def deliver_body(recv, *outs):
    for y in range(4):
        for z in range(4):
            for which, out in enumerate(outs):
                out[0, z * 16 : z * 16 + 16, y * 128 : y * 128 + 128] = recv[y * 4 + z, which]


def deliver(recv):
    out = jax.ShapeDtypeStruct((1, 64, 512), jnp.float32)
    return call(deliver_body, out_shape=(out, out), name="deliver")(recv)


def shards(right_side, affinity_blocks, block_coords, block_counts):
    r = lax.axis_index("row")
    c = lax.axis_index("col")
    yh, yl, z, k = r // 4, c // 8, (c // 2) % 4, c % 2
    own0, own1 = halves(affinity_blocks)
    left0 = lax.ppermute(own0, RC, shift_y(1))
    right1 = lax.ppermute(own1, RC, shift_y(3))

    br = block_coords[:, 0, :, 0]
    bc = block_coords[:, 0, :, 1]
    par = jnp.arange(2, dtype=jnp.int32)[:, None] ^ k
    row128 = par * 8 + ((br // 2) * 2 + yh) * 2 + br % 2
    col128 = ((bc // 2) * 2 + yl) * 2 + bc % 2
    live = jnp.arange(8, dtype=jnp.int32)[None, :] < block_counts
    code = jnp.where(live, row128 * 8 + col128, -1).astype(jnp.float32)
    meta = jnp.pad(code.reshape(1, 16), ((0, 7), (0, 112)))

    send = right_side.reshape(4, 16, 4, 128).transpose(2, 0, 1, 3).reshape(16, 16, 128)
    send = jnp.concatenate([send, jnp.broadcast_to(meta[None], (16, 8, 128))], axis=1)
    recv = exchange(send, SHEETS)
    codes = lax.dynamic_slice(recv.reshape(4, 4, 24, 128), (0, z, 16, 0), (4, 1, 1, 16))
    codes = jnp.concatenate(
        [codes.reshape(64).astype(jnp.int32), jnp.stack([yh * 2 + yl, k]).astype(jnp.int32)]
    )

    wave, back = pack(left0, own1, right1, own0, recv)
    send, sums = start(recv)
    state = (recv,)
    wave = lax.ppermute(wave, RC, shift_y(1))
    back = lax.ppermute(back, RC, shift_y(3))
    got = exchange(send, PLANES)
    hi, lo, share = early(codes, own0, own1, left0, right1, got)
    hi, lo = late(codes, wave, back, hi, lo)
    for step in range(ITERS):
        if step:
            got = share = exchange(send, PLANES)
        products = exchange(multiply(got, share, sums, hi, lo), PLANES)
        made = update(step, products, *state)
        if step + 1 < ITERS:
            send, sums = made[0], made[6]
            state = made[1:6]
    done = exchange(made[0], SHEETS)
    return tuple(deliver(done))


def solution(mesh):
    in_specs = (
        P("col", "row", None),
        P("row", "col", None, None, None),
        P("row", "col", None, None),
        P("row", "col"),
    )
    out_specs = (P("col", "row", None), P("col", "row", None))
    return jax.shard_map(
        shards, mesh=mesh, in_specs=in_specs, out_specs=out_specs, check_vma=False
    )
```

```python
import functools

import jax
import jax.numpy as jnp
from jax import lax
from jax.experimental import pallas as pl
from jax.experimental.pallas import tpu as pltpu
from jax.sharding import PartitionSpec as P

ITERS = 3
DIFFUSION = 0.8
RC = ("row", "col")


def split_id(device):
    r, c = divmod(device, 16)
    yh, x = divmod(r, 4)
    yl, q = divmod(c, 8)
    return yh * 2 + yl, x, q // 2, q % 2


def device_id(y, x, z, k):
    return ((y // 2) * 4 + x) * 16 + (y % 2) * 8 + z * 2 + k


def groups_by(key):
    groups = {}
    for device in range(128):
        groups.setdefault(key(*split_id(device)), []).append(device)
    return list(groups.values())


PLANES = groups_by(lambda y, x, z, k: (y, k))
SHEETS = groups_by(lambda y, x, z, k: (x, k))


def shift_y(d):
    pairs = []
    for device in range(128):
        y, x, z, k = split_id(device)
        pairs.append((device, device_id((y + d) % 4, x, z, k)))
    return pairs


SWAP = [(device, device ^ 1) for device in range(128)]


def exchange(send, groups):
    return lax.all_to_all(send, RC, 0, 0, axis_index_groups=groups, tiled=True)


def call(body, limit=16, **kw):
    return pl.pallas_call(
        body, compiler_params=pltpu.CompilerParams(vmem_limit_bytes=limit * 2**20), **kw
    )


EARLY = ((0, 0), (0, 1), (1, 0), (3, 1))
LATE = ((2, 0), (1, 1), (2, 1), (3, 0))


def corners(codes, back, half):
    y = (codes[64] - back) & 3
    row = (half ^ codes[65]) * 1024 + (y >> 1) * 256
    col = (y & 1) * 256
    for j in range(2):
        for i in range(2):
            at = pl.ds(pl.multiple_of(row + j * 512, 256), 256)
            by = pl.ds(pl.multiple_of(col + i * 512, 256), 256)
            yield j, i, at, by


def fill(codes, ref, first, back, half, hi, lo, work):
    work[...] = jnp.zeros_like(work)
    base = ((codes[64] - back) & 3) * 16 + half * 8
    for b in range(8):
        code = codes[base + b]

        @pl.when(code >= 0)
        def _(b=b, code=code):
            row, col = code >> 3, code & 7
            ro = pl.multiple_of((((row >> 2) & 1) * 2 + (row & 1)) * 128, 128)
            co = pl.multiple_of(((col >> 2) * 2 + (col & 1)) * 128, 128)
            work[pl.ds(ro, 128), pl.ds(co, 128)] += ref[first + b]

    for j, i, at, by in corners(codes, back, half):
        top, rest = parted(work[j * 256 : (j + 1) * 256, i * 256 : (i + 1) * 256])
        hi[at, by] = top
        lo[at, by] = rest


def early_body(codes, own0, own1, left0, right1, recv, hi, lo, share, work):
    share[...] = recv[:, :64, :]
    for ref, place in zip((own0, own1, left0, right1), EARLY):
        fill(codes, ref, 0, *place, hi, lo, work)


def late_body(codes, wave_in, back_in, hi0, lo0, hi, lo, work, wave, back, sems):
    copies = (
        pltpu.make_async_copy(wave_in, wave, sems.at[0]),
        pltpu.make_async_copy(back_in, back, sems.at[1]),
    )
    for copy in copies:
        copy.start()
    for place in EARLY:
        for _, _, at, by in corners(codes, *place):
            hi[at, by] = hi0[at, by]
            lo[at, by] = lo0[at, by]
    copies[0].wait()
    fill(codes, wave, 0, *LATE[0], hi, lo, work)
    fill(codes, wave, 8, *LATE[1], hi, lo, work)
    copies[1].wait()
    fill(codes, back, 0, *LATE[2], hi, lo, work)
    fill(codes, back, 8, *LATE[3], hi, lo, work)


VMEM = pl.BlockSpec(memory_space=pltpu.VMEM)
HBM = pl.BlockSpec(memory_space=pltpu.HBM)


SMEM = pl.BlockSpec(memory_space=pltpu.SMEM)
HALF = jax.ShapeDtypeStruct((2048, 1024), jnp.bfloat16)


def early(codes, *operands):
    return call(
        early_body,
        out_shape=(HALF, HALF, jax.ShapeDtypeStruct((16, 64, 128), jnp.float32)),
        in_specs=[SMEM] + [VMEM] * 5,
        out_specs=(VMEM,) * 3,
        scratch_shapes=[pltpu.VMEM((512, 512), jnp.float32)],
        name="early",
    )(codes, *operands)


def late(codes, *operands):
    return call(
        late_body,
        out_shape=(HALF, HALF),
        in_specs=[SMEM, HBM, HBM, VMEM, VMEM],
        out_specs=(VMEM,) * 2,
        scratch_shapes=[pltpu.VMEM((512, 512), jnp.float32)]
        + [pltpu.VMEM((16, 128, 128), jnp.float32)] * 2
        + [pltpu.SemaphoreType.DMA((2,))],
        name="late",
    )(codes, *operands)


def parted(value):
    top = value.astype(jnp.bfloat16)
    return top, (value - top.astype(jnp.float32)).astype(jnp.bfloat16)


def dot(a, b):
    return jnp.dot(a, b, preferred_element_type=jnp.float32)


def chunk(ref, j):
    return ref[:, j * 16 : j * 16 + 16, :].reshape(256, 128)


def part_right(recv, right):
    for s in range(4):
        top, rest = parted(chunk(recv, 4 + s))
        right[pl.ds(s * 256, 256), :128] = top
        right[pl.ds(s * 256, 256), 128:] = rest


def forward(hi, lo, right):
    wide = dot(hi, right[...])
    return wide[:, :128] + wide[:, 128:] + dot(lo, right[:, :128])


def mate_body(recv, hi, lo, out, right):
    part_right(recv, right)
    for i in range(2):
        rows = slice(1024 + i * 512, 1536 + i * 512)
        out[i * 512 : (i + 1) * 512, :] = forward(hi[rows, :], lo[rows, :], right)


def mate(recv, hi, lo):
    return call(
        mate_body,
        out_shape=jax.ShapeDtypeStruct((1024, 128), jnp.float32),
        in_specs=[VMEM] * 3,
        out_specs=VMEM,
        scratch_shapes=[pltpu.VMEM((1024, 256), jnp.bfloat16)],
        name="mate",
    )(recv, hi, lo)


def mirror_body(recv, other, hi, lo, sums, after, out, scalars, back):
    for i in range(4):
        ref = (recv, other)[i // 2]
        pairs = [parted(chunk(ref, (i % 2) * 2 + c).T) for c in range(2)]
        top = jnp.concatenate([pair[0] for pair in pairs], axis=1)
        rest = jnp.concatenate([pair[1] for pair in pairs], axis=1)
        rows = slice(i * 512, (i + 1) * 512)
        wide = dot(jnp.concatenate([top, rest], axis=0), hi[rows, :])
        part = wide[:128] + wide[128:] + dot(top, lo[rows, :])
        back[...] = part if i == 0 else back[...] + part
    out[...] = back[...].T
    curve = jnp.zeros((8, 128), jnp.float32)
    for s in range(4):
        piece = chunk(recv, 4 + s) * out[s * 256 : (s + 1) * 256]
        curve = curve + jnp.sum(piece.reshape(32, 8, 128), axis=0)
    place = lax.broadcasted_iota(jnp.int32, (8, 128), 0)
    scalars[...] = jnp.where(place == 2, row_sum(curve) * (2 * DIFFUSION), sums[...])


def mirror(recv, other, hi, lo, sums, after):
    return call(
        mirror_body,
        out_shape=(
            jax.ShapeDtypeStruct((1024, 128), jnp.float32),
            jax.ShapeDtypeStruct((8, 128), jnp.float32),
        ),
        in_specs=[VMEM] * 6,
        out_specs=(VMEM, VMEM),
        scratch_shapes=[pltpu.VMEM((128, 1024), jnp.float32)],
        name="mirror",
    )(recv, other, hi, lo, sums, after)


def own_body(first, recv, hi, lo, after, out, right):
    part_right(recv, right)
    rows = slice(first, first + 512)
    out[...] = forward(hi[rows, :], lo[rows, :], right)


def own_rows(first, recv, hi, lo, after):
    return call(
        functools.partial(own_body, first),
        out_shape=jax.ShapeDtypeStruct((512, 128), jnp.float32),
        in_specs=[VMEM] * 4,
        out_specs=VMEM,
        scratch_shapes=[pltpu.VMEM((1024, 256), jnp.bfloat16)],
        name="own_rows",
    )(recv, hi, lo, after)


def join_body(ours0, ours1, theirs, mirrored, mine, mates, out):
    for s in range(4):
        rows = slice(s * 256, (s + 1) * 256)
        ours = (ours0, ours1)[s // 2]
        part = ours[(s % 2) * 256 : (s % 2) * 256 + 256, :] + theirs[rows, :]
        out[:, s * 16 : s * 16 + 16, :] = part.reshape(16, 16, 128)
        out[:, 64 + s * 16 : 80 + s * 16, :] = mirrored[rows, :].reshape(16, 16, 128)
    row = mine[...] + mates[...]
    out[:, 128:136, :] = jnp.broadcast_to(row[None], (16, 8, 128))


def join(ours0, ours1, theirs, mirrored, mine, mates):
    return call(
        join_body,
        out_shape=jax.ShapeDtypeStruct((16, 136, 128), jnp.float32),
        in_specs=[VMEM] * 6,
        out_specs=VMEM,
        name="join",
    )(ours0, ours1, theirs, mirrored, mine, mates)


def multiply(recv, share, sums, hi, lo):
    other = lax.ppermute(share, RC, SWAP)
    part = mate(recv, hi, lo)
    theirs = lax.ppermute(part, RC, SWAP)
    ours0 = own_rows(0, recv, hi, lo, part)
    mirrored, mine = mirror(recv, other, hi, lo, sums, ours0)
    mates = lax.ppermute(mine, RC, SWAP)
    ours1 = own_rows(512, recv, hi, lo, mine)
    return join(ours0, ours1, theirs, mirrored, mine, mates)


def spread(field, send):
    for s in range(4):
        for g in range(4):
            piece = field(s, g)
            for other in range(4):
                send[g * 4 + other, s * 16 : s * 16 + 16, :] = piece
                send[other * 4 + g, 64 + s * 16 : 80 + s * 16, :] = piece


def row_sum(value):
    return jnp.sum(value, axis=0, keepdims=True)


def rows_of(*rows):
    place = lax.broadcasted_iota(jnp.int32, (8, 128), 0)
    out = jnp.zeros((8, 128), jnp.float32)
    for i, row in enumerate(rows):
        out = jnp.where(place == i, row, out)
    return out


def halves_body(blocks, own0, own1, sems):
    copies = [
        pltpu.make_async_copy(blocks.at[i, 0], out, sems.at[i])
        for i, out in enumerate((own0, own1))
    ]
    for copy in copies:
        copy.start()
    for copy in copies:
        copy.wait()


def halves(blocks):
    half = jax.ShapeDtypeStruct((8, 128, 128), jnp.float32)
    return call(
        halves_body,
        out_shape=(half, half),
        in_specs=[HBM],
        out_specs=(VMEM, VMEM),
        scratch_shapes=[pltpu.SemaphoreType.DMA((2,))],
        name="halves",
    )(blocks)


def pack_body(passed, kept, recv, wave, sems):
    copies = [
        pltpu.make_async_copy(src, wave.at[pl.ds(first, 8)], sems.at[i])
        for i, (src, first) in enumerate(((passed, 0), (kept, 8)))
    ]
    for copy in copies:
        copy.start()
    for copy in copies:
        copy.wait()


def pack(*operands):
    return call(
        pack_body,
        out_shape=jax.ShapeDtypeStruct((16, 128, 128), jnp.float32),
        in_specs=[VMEM] * 3,
        out_specs=HBM,
        scratch_shapes=[pltpu.SemaphoreType.DMA((2,))],
        name="pack",
    )(*operands)


def start_body(recv, send, sums):
    spread(lambda s, g: recv[s * 4 + g, :16], send)
    square = jnp.zeros((16, 128), jnp.float32)
    for i in range(16):
        piece = recv[i, :16]
        square = square + piece * piece
    sums[...] = rows_of(row_sum(square))


def start(recv):
    big = jax.ShapeDtypeStruct((16, 128, 128), jnp.float32)
    small = jax.ShapeDtypeStruct((8, 128), jnp.float32)
    return call(
        start_body,
        out_shape=(big, small),
        in_specs=[VMEM],
        out_specs=(VMEM, VMEM),
        name="start",
    )(recv)


def update_body(step, *refs):
    if step == 0:
        recv, residual = refs[:2]
        outs = refs[2:]
    else:
        recv, residual, direction, image, ranking, last = refs[:6]
        outs = refs[6:]
    total = jnp.zeros((8, 128), jnp.float32)
    for i in range(16):
        total = total + recv[i, 128:136]
    now = total[0:1]
    curve = now - total[2:3]
    if step > 0:
        beta = now / last[0:1]
        curve = curve + 2.0 * beta * total[1:2] + beta * beta * last[1:2]
    alpha = now / curve
    final = step + 1 == ITERS
    square = jnp.zeros((16, 128), jnp.float32)
    cross = jnp.zeros((16, 128), jnp.float32)
    for s in range(4):
        for g in range(4):
            acc = jnp.zeros((16, 128), jnp.float32)
            for other in range(4):
                acc = acc + recv[g * 4 + other, s * 16 : s * 16 + 16]
                acc = acc + recv[other * 4 + g, 64 + s * 16 : 80 + s * 16]
            i = s * 4 + g
            rest = residual[i, :16]
            aim = rest
            made = rest - DIFFUSION * acc
            if step > 0:
                aim = aim + beta * direction[i]
                made = made + beta * image[i]
            ranked = alpha * aim
            if step > 0:
                ranked = ranked + ranking[i]
            rest = rest - alpha * made
            if final:
                outs[0][i, 0] = ranked
                outs[0][i, 1] = rest
            else:
                send, new_residual, new_direction, new_image, new_ranking = outs[:5]
                new_residual[i] = rest
                new_direction[i] = aim
                new_image[i] = made
                new_ranking[i] = ranked
                square = square + rest * rest
                cross = cross + rest * made
    if not final:
        spread(lambda s, g: new_residual[s * 4 + g], send)
        outs[5][...] = rows_of(now, curve)
        outs[6][...] = rows_of(row_sum(square), row_sum(cross))


def update(step, *operands):
    field = jax.ShapeDtypeStruct((16, 16, 128), jnp.float32)
    small = jax.ShapeDtypeStruct((8, 128), jnp.float32)
    if step + 1 == ITERS:
        shapes = [jax.ShapeDtypeStruct((16, 2, 16, 128), jnp.float32)]
    else:
        send = jax.ShapeDtypeStruct((16, 128, 128), jnp.float32)
        shapes = [send, field, field, field, field, small, small]
    return call(
        functools.partial(update_body, step), out_shape=shapes, name="update"
    )(*operands)


def deliver_body(recv, *outs):
    for y in range(4):
        for z in range(4):
            for which, out in enumerate(outs):
                out[0, z * 16 : z * 16 + 16, y * 128 : y * 128 + 128] = recv[y * 4 + z, which]


def deliver(recv):
    out = jax.ShapeDtypeStruct((1, 64, 512), jnp.float32)
    return call(deliver_body, out_shape=(out, out), name="deliver")(recv)


def shards(right_side, affinity_blocks, block_coords, block_counts):
    r = lax.axis_index("row")
    c = lax.axis_index("col")
    yh, yl, z, k = r // 4, c // 8, (c // 2) % 4, c % 2
    own0, own1 = halves(affinity_blocks)
    left0 = lax.ppermute(own0, RC, shift_y(1))
    right1 = lax.ppermute(own1, RC, shift_y(3))

    br = block_coords[:, 0, :, 0]
    bc = block_coords[:, 0, :, 1]
    par = jnp.arange(2, dtype=jnp.int32)[:, None] ^ k
    row128 = par * 8 + ((br // 2) * 2 + yh) * 2 + br % 2
    col128 = ((bc // 2) * 2 + yl) * 2 + bc % 2
    live = jnp.arange(8, dtype=jnp.int32)[None, :] < block_counts
    code = jnp.where(live, row128 * 8 + col128, -1).astype(jnp.float32)
    meta = jnp.pad(code.reshape(1, 16), ((0, 7), (0, 112)))

    send = right_side.reshape(4, 16, 4, 128).transpose(2, 0, 1, 3).reshape(16, 16, 128)
    send = jnp.concatenate([send, jnp.broadcast_to(meta[None], (16, 8, 128))], axis=1)
    recv = exchange(send, SHEETS)
    codes = lax.dynamic_slice(recv.reshape(4, 4, 24, 128), (0, z, 16, 0), (4, 1, 1, 16))
    codes = jnp.concatenate(
        [codes.reshape(64).astype(jnp.int32), jnp.stack([yh * 2 + yl, k]).astype(jnp.int32)]
    )

    wave = pack(left0, own1, recv)
    back = pack(right1, own0, recv)
    send, sums = start(recv)
    state = (recv,)
    wave = lax.ppermute(wave, RC, shift_y(1))
    back = lax.ppermute(back, RC, shift_y(3))
    got = exchange(send, PLANES)
    hi, lo, share = early(codes, own0, own1, left0, right1, got)
    hi, lo = late(codes, wave, back, hi, lo)
    for step in range(ITERS):
        if step:
            got = share = exchange(send, PLANES)
        products = exchange(multiply(got, share, sums, hi, lo), PLANES)
        made = update(step, products, *state)
        if step + 1 < ITERS:
            send, sums = made[0], made[6]
            state = made[1:6]
    done = exchange(made[0], SHEETS)
    return tuple(deliver(done))


def solution(mesh):
    in_specs = (
        P("col", "row", None),
        P("row", "col", None, None, None),
        P("row", "col", None, None),
        P("row", "col"),
    )
    out_specs = (P("col", "row", None), P("col", "row", None))
    return jax.shard_map(
        shards, mesh=mesh, in_specs=in_specs, out_specs=out_specs, check_vma=False
    )
```

```python
import functools

import jax
import jax.numpy as jnp
from jax import lax
from jax.experimental import pallas as pl
from jax.experimental.pallas import tpu as pltpu
from jax.sharding import PartitionSpec as P

ITERS = 3
DIFFUSION = 0.8
RC = ("row", "col")


def split_id(device):
    r, c = divmod(device, 16)
    yh, x = divmod(r, 4)
    yl, q = divmod(c, 8)
    return yh * 2 + yl, x, q // 2, q % 2


def device_id(y, x, z, k):
    return ((y // 2) * 4 + x) * 16 + (y % 2) * 8 + z * 2 + k


def groups_by(key):
    groups = {}
    for device in range(128):
        groups.setdefault(key(*split_id(device)), []).append(device)
    return list(groups.values())


PLANES = groups_by(lambda y, x, z, k: (y, k))
SHEETS = groups_by(lambda y, x, z, k: (x, k))


def shift_y(d):
    pairs = []
    for device in range(128):
        y, x, z, k = split_id(device)
        pairs.append((device, device_id((y + d) % 4, x, z, k)))
    return pairs


SWAP = [(device, device ^ 1) for device in range(128)]


def exchange(send, groups):
    return lax.all_to_all(send, RC, 0, 0, axis_index_groups=groups, tiled=True)


def call(body, limit=10, **kw):
    return pl.pallas_call(
        body, compiler_params=pltpu.CompilerParams(vmem_limit_bytes=limit * 2**20), **kw
    )


EARLY = ((0, 0), (0, 1), (1, 0), (3, 1))
LATE = ((2, 0), (1, 1), (2, 1), (3, 0))


def corners(codes, back, half):
    y = (codes[64] - back) & 3
    row = (half ^ codes[65]) * 1024 + (y >> 1) * 256
    col = (y & 1) * 256
    for j in range(2):
        for i in range(2):
            at = pl.ds(pl.multiple_of(row + j * 512, 256), 256)
            by = pl.ds(pl.multiple_of(col + i * 512, 256), 256)
            yield j, i, at, by


def fill(codes, ref, first, back, half, hi, lo, work):
    work[...] = jnp.zeros_like(work)
    base = ((codes[64] - back) & 3) * 16 + half * 8
    for b in range(8):
        code = codes[base + b]

        @pl.when(code >= 0)
        def _(b=b, code=code):
            row, col = code >> 3, code & 7
            ro = pl.multiple_of((((row >> 2) & 1) * 2 + (row & 1)) * 128, 128)
            co = pl.multiple_of(((col >> 2) * 2 + (col & 1)) * 128, 128)
            work[pl.ds(ro, 128), pl.ds(co, 128)] += ref[first + b]

    for j, i, at, by in corners(codes, back, half):
        top, rest = parted(work[j * 256 : (j + 1) * 256, i * 256 : (i + 1) * 256])
        hi[at, by] = top
        lo[at, by] = rest


def early_body(codes, own0, own1, left0, right1, recv, hi, lo, share, work):
    share[...] = recv[:, :64, :]
    for ref, place in zip((own0, own1, left0, right1), EARLY):
        fill(codes, ref, 0, *place, hi, lo, work)


def late_body(codes, wave_in, back_in, hi0, lo0, hi, lo, work, wave, back, sems):
    copies = (
        pltpu.make_async_copy(wave_in, wave, sems.at[0]),
        pltpu.make_async_copy(back_in, back, sems.at[1]),
    )
    for copy in copies:
        copy.start()
    for place in EARLY:
        for _, _, at, by in corners(codes, *place):
            hi[at, by] = hi0[at, by]
            lo[at, by] = lo0[at, by]
    copies[0].wait()
    fill(codes, wave, 0, *LATE[0], hi, lo, work)
    fill(codes, wave, 8, *LATE[1], hi, lo, work)
    copies[1].wait()
    fill(codes, back, 0, *LATE[2], hi, lo, work)
    fill(codes, back, 8, *LATE[3], hi, lo, work)


VMEM = pl.BlockSpec(memory_space=pltpu.VMEM)
HBM = pl.BlockSpec(memory_space=pltpu.HBM)


SMEM = pl.BlockSpec(memory_space=pltpu.SMEM)
HALF = jax.ShapeDtypeStruct((2048, 1024), jnp.bfloat16)


def early(codes, *operands):
    return call(
        early_body,
        out_shape=(HALF, HALF, jax.ShapeDtypeStruct((16, 64, 128), jnp.float32)),
        in_specs=[SMEM] + [VMEM] * 5,
        out_specs=(VMEM,) * 3,
        scratch_shapes=[pltpu.VMEM((512, 512), jnp.float32)],
        name="early",
    )(codes, *operands)


def late(codes, *operands):
    return call(
        late_body,
        out_shape=(HALF, HALF),
        in_specs=[SMEM, HBM, HBM, VMEM, VMEM],
        out_specs=(VMEM,) * 2,
        scratch_shapes=[pltpu.VMEM((512, 512), jnp.float32)]
        + [pltpu.VMEM((16, 128, 128), jnp.float32)] * 2
        + [pltpu.SemaphoreType.DMA((2,))],
        name="late",
    )(codes, *operands)


def parted(value):
    top = value.astype(jnp.bfloat16)
    return top, (value - top.astype(jnp.float32)).astype(jnp.bfloat16)


def dot(a, b):
    return jnp.dot(a, b, preferred_element_type=jnp.float32)


def chunk(ref, j):
    return ref[:, j * 16 : j * 16 + 16, :].reshape(256, 128)


def part_right(recv, right):
    for s in range(4):
        top, rest = parted(chunk(recv, 4 + s))
        right[pl.ds(s * 256, 256), :128] = top
        right[pl.ds(s * 256, 256), 128:] = rest


def forward(hi, lo, right):
    wide = dot(hi, right[...])
    return wide[:, :128] + wide[:, 128:] + dot(lo, right[:, :128])


def mate_body(recv, hi, lo, out, right):
    part_right(recv, right)
    for i in range(2):
        rows = slice(1024 + i * 512, 1536 + i * 512)
        out[i * 512 : (i + 1) * 512, :] = forward(hi[rows, :], lo[rows, :], right)


def mate(recv, hi, lo):
    return call(
        mate_body,
        out_shape=jax.ShapeDtypeStruct((1024, 128), jnp.float32),
        in_specs=[VMEM] * 3,
        out_specs=VMEM,
        scratch_shapes=[pltpu.VMEM((1024, 256), jnp.bfloat16)],
        name="mate",
    )(recv, hi, lo)


def mirror_body(recv, other, hi, lo, sums, after, out, scalars, back):
    for i in range(4):
        ref = (recv, other)[i // 2]
        pairs = [parted(chunk(ref, (i % 2) * 2 + c).T) for c in range(2)]
        top = jnp.concatenate([pair[0] for pair in pairs], axis=1)
        rest = jnp.concatenate([pair[1] for pair in pairs], axis=1)
        rows = slice(i * 512, (i + 1) * 512)
        wide = dot(jnp.concatenate([top, rest], axis=0), hi[rows, :])
        part = wide[:128] + wide[128:] + dot(top, lo[rows, :])
        back[...] = part if i == 0 else back[...] + part
    out[...] = back[...].T
    curve = jnp.zeros((8, 128), jnp.float32)
    for s in range(4):
        piece = chunk(recv, 4 + s) * out[s * 256 : (s + 1) * 256]
        curve = curve + jnp.sum(piece.reshape(32, 8, 128), axis=0)
    place = lax.broadcasted_iota(jnp.int32, (8, 128), 0)
    scalars[...] = jnp.where(place == 2, row_sum(curve) * (2 * DIFFUSION), sums[...])


def mirror(recv, other, hi, lo, sums, after):
    return call(
        mirror_body,
        out_shape=(
            jax.ShapeDtypeStruct((1024, 128), jnp.float32),
            jax.ShapeDtypeStruct((8, 128), jnp.float32),
        ),
        in_specs=[VMEM] * 6,
        out_specs=(VMEM, VMEM),
        scratch_shapes=[pltpu.VMEM((128, 1024), jnp.float32)],
        name="mirror",
    )(recv, other, hi, lo, sums, after)


def own_body(first, recv, hi, lo, after, out, right):
    part_right(recv, right)
    rows = slice(first, first + 512)
    out[...] = forward(hi[rows, :], lo[rows, :], right)


def own_rows(first, recv, hi, lo, after):
    return call(
        functools.partial(own_body, first),
        out_shape=jax.ShapeDtypeStruct((512, 128), jnp.float32),
        in_specs=[VMEM] * 4,
        out_specs=VMEM,
        scratch_shapes=[pltpu.VMEM((1024, 256), jnp.bfloat16)],
        name="own_rows",
    )(recv, hi, lo, after)


def join_body(ours0, ours1, theirs, mirrored, mine, mates, out):
    for s in range(4):
        rows = slice(s * 256, (s + 1) * 256)
        ours = (ours0, ours1)[s // 2]
        part = ours[(s % 2) * 256 : (s % 2) * 256 + 256, :] + theirs[rows, :]
        out[:, s * 16 : s * 16 + 16, :] = part.reshape(16, 16, 128)
        out[:, 64 + s * 16 : 80 + s * 16, :] = mirrored[rows, :].reshape(16, 16, 128)
    row = mine[...] + mates[...]
    out[:, 128:136, :] = jnp.broadcast_to(row[None], (16, 8, 128))


def join(ours0, ours1, theirs, mirrored, mine, mates):
    return call(
        join_body,
        out_shape=jax.ShapeDtypeStruct((16, 136, 128), jnp.float32),
        in_specs=[VMEM] * 6,
        out_specs=VMEM,
        name="join",
    )(ours0, ours1, theirs, mirrored, mine, mates)


def multiply(recv, share, sums, hi, lo):
    other = lax.ppermute(share, RC, SWAP)
    part = mate(recv, hi, lo)
    theirs = lax.ppermute(part, RC, SWAP)
    ours0 = own_rows(0, recv, hi, lo, part)
    mirrored, mine = mirror(recv, other, hi, lo, sums, ours0)
    mates = lax.ppermute(mine, RC, SWAP)
    ours1 = own_rows(512, recv, hi, lo, mine)
    return join(ours0, ours1, theirs, mirrored, mine, mates)


def spread(field, send):
    for s in range(4):
        for g in range(4):
            piece = field(s, g)
            for other in range(4):
                send[g * 4 + other, s * 16 : s * 16 + 16, :] = piece
                send[other * 4 + g, 64 + s * 16 : 80 + s * 16, :] = piece


def row_sum(value):
    return jnp.sum(value, axis=0, keepdims=True)


def rows_of(*rows):
    place = lax.broadcasted_iota(jnp.int32, (8, 128), 0)
    out = jnp.zeros((8, 128), jnp.float32)
    for i, row in enumerate(rows):
        out = jnp.where(place == i, row, out)
    return out


def halves_body(blocks, own0, own1, sems):
    copies = [
        pltpu.make_async_copy(blocks.at[i, 0], out, sems.at[i])
        for i, out in enumerate((own0, own1))
    ]
    for copy in copies:
        copy.start()
    for copy in copies:
        copy.wait()


def halves(blocks):
    half = jax.ShapeDtypeStruct((8, 128, 128), jnp.float32)
    return call(
        halves_body,
        out_shape=(half, half),
        in_specs=[HBM],
        out_specs=(VMEM, VMEM),
        scratch_shapes=[pltpu.SemaphoreType.DMA((2,))],
        name="halves",
    )(blocks)


def pack_body(left0, own1, right1, own0, recv, wave, back, sems):
    pieces = ((left0, wave, 0), (own1, wave, 8), (right1, back, 0), (own0, back, 8))
    copies = [
        pltpu.make_async_copy(src, dst.at[pl.ds(first, 8)], sems.at[i])
        for i, (src, dst, first) in enumerate(pieces)
    ]
    for copy in copies:
        copy.start()
    for copy in copies:
        copy.wait()


def pack(*operands):
    big = jax.ShapeDtypeStruct((16, 128, 128), jnp.float32)
    return call(
        pack_body,
        out_shape=(big, big),
        in_specs=[VMEM] * 5,
        out_specs=(HBM, HBM),
        scratch_shapes=[pltpu.SemaphoreType.DMA((4,))],
        name="pack",
    )(*operands)


def start_body(recv, send, sums):
    spread(lambda s, g: recv[s * 4 + g, :16], send)
    square = jnp.zeros((16, 128), jnp.float32)
    for i in range(16):
        piece = recv[i, :16]
        square = square + piece * piece
    sums[...] = rows_of(row_sum(square))


def start(recv):
    big = jax.ShapeDtypeStruct((16, 128, 128), jnp.float32)
    small = jax.ShapeDtypeStruct((8, 128), jnp.float32)
    return call(
        start_body,
        out_shape=(big, small),
        in_specs=[VMEM],
        out_specs=(VMEM, VMEM),
        name="start",
    )(recv)


def update_body(step, *refs):
    if step == 0:
        recv, residual = refs[:2]
        outs = refs[2:]
    else:
        recv, residual, direction, image, ranking, last = refs[:6]
        outs = refs[6:]
    total = jnp.zeros((8, 128), jnp.float32)
    for i in range(16):
        total = total + recv[i, 128:136]
    now = total[0:1]
    curve = now - total[2:3]
    if step > 0:
        beta = now / last[0:1]
        curve = curve + 2.0 * beta * total[1:2] + beta * beta * last[1:2]
    alpha = now / curve
    final = step + 1 == ITERS
    square = jnp.zeros((16, 128), jnp.float32)
    cross = jnp.zeros((16, 128), jnp.float32)
    for s in range(4):
        for g in range(4):
            acc = jnp.zeros((16, 128), jnp.float32)
            for other in range(4):
                acc = acc + recv[g * 4 + other, s * 16 : s * 16 + 16]
                acc = acc + recv[other * 4 + g, 64 + s * 16 : 80 + s * 16]
            i = s * 4 + g
            rest = residual[i, :16]
            aim = rest
            made = rest - DIFFUSION * acc
            if step > 0:
                aim = aim + beta * direction[i]
                made = made + beta * image[i]
            ranked = alpha * aim
            if step > 0:
                ranked = ranked + ranking[i]
            rest = rest - alpha * made
            if final:
                outs[0][i, 0] = ranked
                outs[0][i, 1] = rest
            else:
                send, new_residual, new_direction, new_image, new_ranking = outs[:5]
                new_residual[i] = rest
                new_direction[i] = aim
                new_image[i] = made
                new_ranking[i] = ranked
                square = square + rest * rest
                cross = cross + rest * made
    if not final:
        spread(lambda s, g: new_residual[s * 4 + g], send)
        outs[5][...] = rows_of(now, curve)
        outs[6][...] = rows_of(row_sum(square), row_sum(cross))


def update(step, *operands):
    field = jax.ShapeDtypeStruct((16, 16, 128), jnp.float32)
    small = jax.ShapeDtypeStruct((8, 128), jnp.float32)
    if step + 1 == ITERS:
        shapes = [jax.ShapeDtypeStruct((16, 2, 16, 128), jnp.float32)]
    else:
        send = jax.ShapeDtypeStruct((16, 128, 128), jnp.float32)
        shapes = [send, field, field, field, field, small, small]
    return call(
        functools.partial(update_body, step), out_shape=shapes, name="update"
    )(*operands)


def deliver_body(recv, *outs):
    for y in range(4):
        for z in range(4):
            for which, out in enumerate(outs):
                out[0, z * 16 : z * 16 + 16, y * 128 : y * 128 + 128] = recv[y * 4 + z, which]


def deliver(recv):
    out = jax.ShapeDtypeStruct((1, 64, 512), jnp.float32)
    return call(deliver_body, out_shape=(out, out), name="deliver")(recv)


def shards(right_side, affinity_blocks, block_coords, block_counts):
    r = lax.axis_index("row")
    c = lax.axis_index("col")
    yh, yl, z, k = r // 4, c // 8, (c // 2) % 4, c % 2
    own0, own1 = halves(affinity_blocks)
    left0 = lax.ppermute(own0, RC, shift_y(1))
    right1 = lax.ppermute(own1, RC, shift_y(3))

    br = block_coords[:, 0, :, 0]
    bc = block_coords[:, 0, :, 1]
    par = jnp.arange(2, dtype=jnp.int32)[:, None] ^ k
    row128 = par * 8 + ((br // 2) * 2 + yh) * 2 + br % 2
    col128 = ((bc // 2) * 2 + yl) * 2 + bc % 2
    live = jnp.arange(8, dtype=jnp.int32)[None, :] < block_counts
    code = jnp.where(live, row128 * 8 + col128, -1).astype(jnp.float32)
    meta = jnp.pad(code.reshape(1, 16), ((0, 7), (0, 112)))

    send = right_side.reshape(4, 16, 4, 128).transpose(2, 0, 1, 3).reshape(16, 16, 128)
    send = jnp.concatenate([send, jnp.broadcast_to(meta[None], (16, 8, 128))], axis=1)
    recv = exchange(send, SHEETS)
    codes = lax.dynamic_slice(recv.reshape(4, 4, 24, 128), (0, z, 16, 0), (4, 1, 1, 16))
    codes = jnp.concatenate(
        [codes.reshape(64).astype(jnp.int32), jnp.stack([yh * 2 + yl, k]).astype(jnp.int32)]
    )

    wave, back = pack(left0, own1, right1, own0, recv)
    send, sums = start(recv)
    state = (recv,)
    wave = lax.ppermute(wave, RC, shift_y(1))
    back = lax.ppermute(back, RC, shift_y(3))
    got = exchange(send, PLANES)
    hi, lo, share = early(codes, own0, own1, left0, right1, got)
    hi, lo = late(codes, wave, back, hi, lo)
    for step in range(ITERS):
        if step:
            got = share = exchange(send, PLANES)
        products = exchange(multiply(got, share, sums, hi, lo), PLANES)
        made = update(step, products, *state)
        if step + 1 < ITERS:
            send, sums = made[0], made[6]
            state = made[1:6]
    done = exchange(made[0], SHEETS)
    return tuple(deliver(done))


def solution(mesh):
    in_specs = (
        P("col", "row", None),
        P("row", "col", None, None, None),
        P("row", "col", None, None),
        P("row", "col"),
    )
    out_specs = (P("col", "row", None), P("col", "row", None))
    return jax.shard_map(
        shards, mesh=mesh, in_specs=in_specs, out_specs=out_specs, check_vma=False
    )
```
